32 devices in a mesh: groups: 2 (over y), seq: 4 (over z), blk: 2 (over x), chan: 2 (over core).
Axes of the slice: x: 2, y: 2, z: 4, core: 2. Of those that a mesh axis runs over, the one named last changes fastest.
Arguments:
- queries: bfloat16 [4, 8, 32, 4096], P(('groups', 'blk'), 'seq', 'chan'), parts along dimension 0, may hold values from -8 to 8
- keys: bfloat16 [4, 8, 32, 4096], P(('groups', 'blk'), 'seq', 'chan'), parts along dimension 0, may hold values from -8 to 8
- values: bfloat16 [4, 8, 32, 4096], P(('groups', 'blk'), 'seq', 'chan'), parts along dimension 0, may hold values from -16 to 16
- norm_gain: float32 [4096], replicated, may hold values from 0.1 to 1.9
- head_weight: bfloat16 [4096, 64], replicated, may hold values from -0.09375 to 0.09375
- head_bias: float32 [64], replicated, may hold values from -3 to 3
- in_weight: bfloat16 [3, 3, 64, 512], replicated, may hold values from -0.25 to 0.25
- in_bias: float32 [512], replicated, may hold values from -3 to 3
- conv_weight: bfloat16 [3, 3, 512, 512], P(None, None, None, 'chan'), may hold values from -0.15625 to 0.15625
- conv_bias: float32 [512], P('chan'), may hold values from -3 to 3
Outputs:
- decoded: bfloat16 [4, 8, 32, 512], P(('groups', 'blk'), 'seq', None, 'chan'), parts along dimension 0
The draws below stay inside these ranges and needn't reach their ends.
There are 2 independent parts, one for each index of `groups`. The reference program is written for one: setup_inputs(seed, part) draws one part's arguments, and reference() takes and returns one part's arrays. A program takes and returns all parts, laid end to end along the dimension named above; an argument that names none is the same for every part. Nothing has to cross between parts.
All inputs are finite; a program needn't handle non-finite values.
Results may differ from the reference program's by a relative error of at most 0.025.
Values may be sent and summed in bfloat16 or wider, within the bound.
No kernel may reach another device: no remote copies, remote signals or barrier semaphores. Data moves between devices by JAX's collectives and lax.ppermute only.
A program may use at most 64 MiB of HBM per device.

```python
import jax
import jax.numpy as jnp
from jax import lax

HD = 128
HEADS = 32
LAT = 64
WIDE = 512
COLS = 32
FEAT = 4096
FRAMES = 2
ROWS = 8


def shared_draw(key):
    key_query, key_keys = jax.random.split(jax.random.fold_in(key, 7), 2)
    token_count = FRAMES * ROWS * COLS
    shape = (token_count, FEAT)
    query_rows = jnp.clip(jax.random.normal(key_query, shape, jnp.float32), -8.0, 8.0)
    key_rows = jnp.clip(jax.random.normal(key_keys, shape, jnp.float32), -8.0, 8.0)
    return (query_rows.reshape(FRAMES, ROWS, COLS, FEAT), key_rows.reshape(FRAMES, ROWS, COLS, FEAT))


def draw_queries(key, part):
    return shared_draw(key)[0].astype(jnp.bfloat16)


def draw_keys(key, part):
    return shared_draw(key)[1].astype(jnp.bfloat16)


def draw_values(key, part):
    key_main = jax.random.fold_in(jax.random.fold_in(key, 11), 0)
    token_count = FRAMES * ROWS * COLS
    base = jax.random.normal(key_main, (token_count, HEADS, HD), jnp.float32)
    head_scale = 3.0 ** (jnp.arange(HEADS, dtype=jnp.float32) / max(HEADS - 1, 1))
    drawn = base * head_scale[None, :, None]
    drawn = jnp.clip(drawn, -16.0, 16.0)
    return drawn.reshape(FRAMES, ROWS, COLS, FEAT).astype(jnp.bfloat16)


def shard_levels(stream_key, dims, shards, smallest, high):
    loudness = 1.0
    for dim, shards_of in shards:
        draws = jax.random.uniform(jax.random.fold_in(jax.random.fold_in(stream_key, 6), dim), (shards_of,), jnp.float32, smallest / len(shards), high / len(shards))
        loudness = loudness * jnp.repeat(jnp.exp(draws), dims[dim] // shards_of).reshape((-1,) + (1,) * (len(dims) - 1 - dim))
    return loudness


def normal_values(stream_key, shape, width, reach, cuts=(), kind=jnp.bfloat16):
    gain = shard_levels(stream_key, shape, cuts, -0.22, 0.18) if cuts else 1.0
    values = jax.random.normal(stream_key, shape, jnp.float32) * width * gain
    return jnp.minimum(jnp.maximum(values, -reach), reach).astype(kind)


def setup_inputs(seed: int = 0, part: int = 0) -> dict:
    seeds = jax.random.split(jax.random.key(seed), 11)
    part_splits = jax.random.split(jax.random.fold_in(seeds[10], part), 11)
    return {
        "queries": draw_queries(jax.random.fold_in(jax.random.fold_in(seeds[10], part), 71), part),
        "keys": draw_keys(jax.random.fold_in(jax.random.fold_in(seeds[10], part), 71), part),
        "values": draw_values(jax.random.fold_in(jax.random.fold_in(seeds[10], part), 71), part),
        "norm_gain": jnp.clip(1.0 + 0.18 * jax.random.normal(seeds[3], (FEAT,), jnp.float32), 0.1, 1.9),
        "head_weight": normal_values(seeds[4], (FEAT, LAT), FEAT ** -0.5, 0.09375),
        "head_bias": normal_values(seeds[5], (LAT,), 0.5, 3.0, (), jnp.float32),
        "in_weight": normal_values(seeds[6], (3, 3, LAT, WIDE), (9 * LAT) ** -0.5, 0.25),
        "in_bias": normal_values(seeds[7], (WIDE,), 0.5, 3.0, (), jnp.float32),
        "conv_weight": normal_values(seeds[8], (3, 3, WIDE, WIDE), (3 * WIDE) ** -0.5, 0.15625, ((3, 2),)),
        "conv_bias": normal_values(seeds[9], (WIDE,), 0.5, 3.0, ((0, 2),), jnp.float32),
    }


epsilon = 1e-06

def conv_frame(inputs, kernel):
    padded = jnp.pad(inputs, ((0, 0), (1, 1), (1, 1), (0, 0)))
    frame_count, row_count, col_count, _ = inputs.shape
    result = jnp.zeros((frame_count * row_count * col_count, kernel.shape[3]), jnp.float32)
    for row_tap in range(3):
        for col_tap in range(3):
            window = padded[:, row_tap:row_tap + row_count, col_tap:col_tap + col_count, :]
            flat = window.reshape(-1, inputs.shape[3])
            result = result + jnp.dot(flat, kernel[row_tap, col_tap], preferred_element_type=jnp.float32)
    return result.reshape(frame_count, row_count, col_count, kernel.shape[3])

def reference(queries, keys, values, norm_gain, head_weight, head_bias, in_weight, in_bias, conv_weight, conv_bias):
    token_count = FRAMES * ROWS * COLS
    score_scale = HD ** (-0.5)
    query_heads = queries.reshape(token_count, HEADS, HD).transpose(1, 0, 2)
    key_heads = keys.reshape(token_count, HEADS, HD).transpose(1, 0, 2)
    value_heads = values.reshape(token_count, HEADS, HD).transpose(1, 0, 2)

    def one_head(triple):
        query_head, key_head, value_head = triple
        scores = jnp.dot(query_head, key_head.T, preferred_element_type=jnp.float32) * score_scale
        row_max = lax.optimization_barrier(jnp.max(scores, axis=-1, keepdims=True))
        expo = jnp.exp(scores - row_max)
        denoms = lax.optimization_barrier(jnp.sum(expo, axis=-1))
        numers = jnp.dot(expo.astype(jnp.bfloat16), value_head, preferred_element_type=jnp.float32)
        return (numers / denoms[:, None]).astype(jnp.bfloat16)
    attended = lax.map(one_head, (query_heads, key_heads, value_heads))
    attended = attended.transpose(1, 0, 2).reshape(token_count, FEAT)
    wide_att = attended.astype(jnp.float32)
    rms = jnp.sqrt(lax.optimization_barrier(jnp.mean(wide_att * wide_att, axis=-1)) + epsilon)
    normed = (wide_att * norm_gain).astype(jnp.bfloat16)
    projected = jnp.dot(normed, head_weight, preferred_element_type=jnp.float32)
    latent = (projected / rms[:, None] + head_bias).astype(jnp.bfloat16)
    latent = latent.reshape(FRAMES, ROWS, COLS, LAT)
    activation = jax.nn.silu(conv_frame(latent, in_weight) + in_bias).astype(jnp.bfloat16)
    decoded = (conv_frame(activation, conv_weight) + conv_bias).astype(jnp.bfloat16)
    return decoded
```

```python
import jax
import jax.numpy as jnp
from jax import lax
from jax.experimental import pallas as pl
from jax.experimental.pallas import tpu as pltpu
from jax.sharding import PartitionSpec as P

HD = 128


epsilon = 1e-06


def with_halo(cells, sides, width):
    for axis, dim in sides:
        count = lax.axis_size(axis)
        ends = count - 1
        head = lax.slice_in_dim(cells, 0, width, axis=dim)
        tail = lax.slice_in_dim(cells, cells.shape[dim] - width, cells.shape[dim], axis=dim)
        cells = jnp.concatenate(
            [
                lax.ppermute(tail, axis, [(i, (i + 1) % count) for i in range(ends)]),
                cells,
                lax.ppermute(head, axis, [((i + 1) % count, i) for i in range(ends)]),
            ],
            axis=dim,
        )
    return cells


def conv_valid(inputs, kernel):
    col_count = inputs.shape[2]
    padded = jnp.pad(inputs, ((0, 0), (0, 0), (1, 1), (0, 0)))
    stacked = jnp.concatenate(
        [padded[:, :, col_tap : col_tap + col_count, :] for col_tap in range(3)], axis=-1
    )
    rows_out = inputs.shape[1] - 2
    result = None
    for row_tap in range(3):
        flat_kernel = kernel[row_tap].reshape(3 * kernel.shape[2], kernel.shape[3])
        term = jnp.einsum(
            "frci,io->frco",
            stacked[:, row_tap : row_tap + rows_out],
            flat_kernel,
            preferred_element_type=jnp.float32,
        )
        result = term if result is None else result + term
    return result


def absorb(running, key_block, value_block, query_heads, score_scale):
    run_max, denoms, numers = running
    scores = (
        jnp.einsum("hqd,hkd->hqk", query_heads, key_block, preferred_element_type=jnp.float32)
        * score_scale
    )
    fresh_max = jnp.maximum(run_max, jnp.max(scores, axis=-1))
    rescale = jnp.exp(run_max - fresh_max)
    expo = jnp.exp(scores - fresh_max[..., None])
    denoms = denoms * rescale + jnp.sum(expo, axis=-1)
    numers = numers * rescale[..., None] + jnp.einsum(
        "hqk,hkd->hqd", expo.astype(jnp.bfloat16), value_block, preferred_element_type=jnp.float32
    )
    return (fresh_max, denoms, numers)


def decode(wide_rows, rows_dev, in_weight, in_bias, conv_weight, conv_bias):
    pre_act = conv_valid(wide_rows, in_weight) + in_bias
    row_ids = lax.axis_index("seq") * rows_dev - 1 + jnp.arange(rows_dev + 2, dtype=jnp.int32)
    inside = (row_ids >= 0) & (row_ids < rows_dev * lax.axis_size("seq"))
    activation = jnp.where(inside[None, :, None, None], jax.nn.silu(pre_act), 0.0).astype(
        jnp.bfloat16
    )
    return (conv_valid(activation, conv_weight) + conv_bias).astype(jnp.bfloat16)


def gathered(
    queries,
    keys,
    values,
    norm_gain,
    head_weight,
    head_bias,
    in_weight,
    in_bias,
    conv_weight,
    conv_bias,
):
    frame_dev, rows_dev, cols_dev, feat = queries.shape
    seq_count = lax.axis_size("seq")
    feat_dev = feat // seq_count
    heads_dev = feat_dev // HD
    score_scale = HD ** (-0.5)
    query_all, key_all, value_all = (
        lax.all_to_all(queries, "seq", split_axis=3, concat_axis=1, tiled=True),
        lax.all_to_all(keys, "seq", split_axis=3, concat_axis=1, tiled=True),
        lax.all_to_all(values, "seq", split_axis=3, concat_axis=1, tiled=True),
    )
    all_rows = query_all.shape[1]

    def to_heads(block):
        return block.reshape(-1, heads_dev, HD).transpose(1, 0, 2)

    query_heads = to_heads(query_all)
    key_heads = to_heads(key_all)
    value_heads = to_heads(value_all)
    token_local = query_heads.shape[1]

    def attend_piece(running, block_pair):
        key_piece, value_piece = block_pair
        key_rows = key_piece.shape[1]
        if key_rows > 1024 and key_rows % 1024 == 0:
            count = key_rows // 1024
            key_split = key_piece.reshape(heads_dev, count, 1024, HD).transpose(1, 0, 2, 3)
            value_split = value_piece.reshape(heads_dev, count, 1024, HD).transpose(1, 0, 2, 3)

            def step_block(state, pair_block):
                return (absorb(state, pair_block[0], pair_block[1], query_heads, score_scale), None)

            running, _ = lax.scan(step_block, running, (key_split, value_split))
            return running
        return absorb(running, key_piece, value_piece, query_heads, score_scale)

    start_state = (
        jnp.full((heads_dev, token_local), -1e30, jnp.float32),
        jnp.zeros((heads_dev, token_local), jnp.float32),
        jnp.zeros((heads_dev, token_local, HD), jnp.float32),
    )
    run_max, denoms, numers = attend_piece(
        start_state,
        (
            lax.all_gather(key_heads, ("blk", "chan"), axis=1, tiled=True),
            lax.all_gather(value_heads, ("blk", "chan"), axis=1, tiled=True),
        ),
    )
    attended = (numers / denoms[..., None]).astype(jnp.bfloat16)
    attended = attended.transpose(1, 0, 2).reshape(frame_dev, all_rows, cols_dev, feat_dev)
    back = lax.all_to_all(attended, "seq", split_axis=1, concat_axis=3, tiled=True)
    wide_att = back.astype(jnp.float32)
    squares = jnp.sum(wide_att * wide_att, axis=-1)
    normed = (wide_att * norm_gain).astype(jnp.bfloat16)
    projected = jnp.einsum("frcd,dl->frcl", normed, head_weight, preferred_element_type=jnp.float32)
    rms = jnp.sqrt(squares / feat + epsilon)
    latent_cols = (projected / rms[..., None] + head_bias).astype(jnp.bfloat16)
    latent = lax.all_gather(latent_cols, "chan", axis=2, tiled=True)
    wide_rows = with_halo(latent, (("seq", 1),), 2)
    return decode(wide_rows, rows_dev, in_weight, in_bias, conv_weight, conv_bias)


def xor_pairs(seq_count, blk_count, row_flip, blk_flip):
    return [
        (s * blk_count + b, (s ^ row_flip) * blk_count + (b ^ blk_flip))
        for s in range(seq_count)
        for b in range(blk_count)
    ]


def pack_kernel(tokens, width, flips, blk_count, queries, keys, values, *rest):
    outs, sems = rest[:-1], rest[-1]
    row = lax.axis_index("seq")
    blk = lax.axis_index("blk")
    copies = []
    for place, (row_flip, blk_flip) in enumerate(flips):
        target = (row ^ row_flip) * blk_count + (blk ^ blk_flip)
        start = pl.multiple_of(target * width, 128)
        for part, source in enumerate((queries, keys, values)):
            copy = pltpu.make_async_copy(
                source.at[:, pl.ds(start, width)],
                outs[place].at[pl.ds(part * tokens, tokens), :],
                sems.at[place * 3 + part],
            )
            copy.start()
            copies.append(copy)
    for copy in copies:
        copy.wait()


def split_square(total, lanes, lane):
    high = total.astype(jnp.bfloat16).astype(jnp.float32)
    return jnp.where(lane == lanes, high, total - high)


def attend_kernel(tokens, width, count, keep, lat, blk_count, *refs):
    own = refs[:count]
    other = refs[count : 2 * count]
    head_t, gain, kept, sent, weight, sem = refs[2 * count :]
    chip = lax.axis_index("seq") * blk_count + lax.axis_index("blk")
    start = pl.multiple_of(chip * width, 128)
    copy = pltpu.make_async_copy(head_t.at[:, pl.ds(start, width)], weight, sem)
    copy.start()
    copy.wait()
    gains = gain[pl.ds(chip, 1), :]
    factor = HD ** (-0.5) * 1.4426950408889634
    squares = None
    projected = None
    for head in range(width // HD):
        span = slice(head * HD, (head + 1) * HD)
        query = jnp.concatenate([ref[0:tokens, span] for ref in own], axis=0)
        key = jnp.concatenate([ref[tokens : 2 * tokens, span] for ref in own + other], axis=0)
        value = jnp.concatenate([ref[2 * tokens :, span] for ref in own + other], axis=0)
        scores = lax.dot_general(
            query, key, (((1,), (1,)), ((), ())), preferred_element_type=jnp.float32
        )
        top = jnp.max(scores, axis=-1, keepdims=True)
        expo = jnp.exp2((scores - top) * factor)
        denom = jnp.sum(expo, axis=-1, keepdims=True)
        numer = jnp.dot(
            expo.astype(jnp.bfloat16), value, preferred_element_type=jnp.float32
        )
        attended = (numer / denom).astype(jnp.bfloat16).astype(jnp.float32)
        square = jnp.sum(attended * attended, axis=-1, keepdims=True)
        normed = (attended * gains[:, span]).astype(jnp.bfloat16)
        term = lax.dot_general(
            normed, weight[:, span], (((1,), (1,)), ((), ())), preferred_element_type=jnp.float32
        )
        squares = square if squares is None else squares + square
        projected = term if projected is None else projected + term
    wide = jnp.concatenate(
        [projected, jnp.zeros((projected.shape[0], 128 - lat), jnp.float32)], axis=1
    )
    lane = lax.broadcasted_iota(jnp.int32, wide.shape, 1)
    edge = keep * tokens
    kept[...] = jnp.where(lane == lat, squares, wide)[:edge].reshape(kept.shape)
    pair = split_square(squares, lat, lane)
    mixed = jnp.where((lane == lat) | (lane == lat + 1), pair, wide)
    sent[...] = mixed[edge:].astype(jnp.bfloat16).reshape(sent.shape)


def spread_kernel(lat, seq_count, kept, arrived, own, *rest):
    outs, total = rest[:-1], rest[-1]
    row = lax.axis_index("seq")
    summed = kept[...] + arrived[...].astype(jnp.float32)
    lane = lax.broadcasted_iota(jnp.int32, summed.shape, 2)
    squares = jnp.sum(
        jnp.where((lane == lat) | (lane == lat + 1), summed, 0.0), axis=-1, keepdims=True
    )
    pair = split_square(squares, lat, lane)
    total[...] = jnp.where((lane == lat) | (lane == lat + 1), pair, summed)
    for flip in range(seq_count):
        target = row ^ flip
        for step in range(3):
            source = target + step - 1
            valid = (source >= 0) & (source < seq_count)
            piece = total[jnp.where(valid, source ^ row, 0)]
            piece = jnp.where(valid, piece, 0.0)
            if flip == 0:
                own[step] = piece
            else:
                outs[flip - 1][step] = piece.astype(jnp.bfloat16)


def latent_kernel(lat, feat, seq_count, own, *rest):
    arrived, bias, out = rest[:-2], rest[-2], rest[-1]
    row = lax.axis_index("seq")
    total = own[...]
    for ref in arrived:
        total = total + ref[...].astype(jnp.float32)
    lane = lax.broadcasted_iota(jnp.int32, total.shape, 2)
    squares = jnp.sum(
        jnp.where((lane == lat) | (lane == lat + 1), total, 0.0), axis=-1, keepdims=True
    )
    rms = jnp.sqrt(squares / feat + epsilon)
    latent = total[:, :, :lat] / rms + bias[...]
    place = row - 1 + lax.broadcasted_iota(jnp.int32, latent.shape, 0)
    latent = jnp.where((place >= 0) & (place < seq_count), latent, 0.0)
    out[...] = latent.astype(jnp.bfloat16)


def exchanged(
    queries,
    keys,
    values,
    norm_gain,
    head_weight,
    head_bias,
    in_weight,
    in_bias,
    conv_weight,
    conv_bias,
):
    frame_dev, rows_dev, cols_dev, feat = queries.shape
    seq_count = lax.axis_size("seq")
    blk_count = lax.axis_size("blk")
    lat = head_weight.shape[1]
    tokens = frame_dev * rows_dev * cols_dev
    chips = seq_count * blk_count
    width = feat // chips
    flips = [(s, b) for b in range(blk_count) for s in range(seq_count)]
    vmem = pl.BlockSpec(memory_space=pltpu.VMEM)
    hbm = pl.BlockSpec(memory_space=pl.ANY)
    flat = [part.reshape(tokens, feat) for part in (queries, keys, values)]
    piece = jax.ShapeDtypeStruct((3 * tokens, width), jnp.bfloat16)
    packed = pl.pallas_call(
        lambda *refs: pack_kernel(tokens, width, flips, blk_count, *refs),
        out_shape=[piece] * chips,
        in_specs=[hbm] * 3,
        out_specs=[vmem] * chips,
        scratch_shapes=[pltpu.SemaphoreType.DMA((3 * chips,))],
        name="pack",
    )(*flat)
    order = sorted(range(1, chips), key=lambda i: (-(flips[i][0] >= seq_count // 2), i))
    own = [packed[0]] + [None] * (chips - 1)
    for i in order:
        own[i] = lax.ppermute(
            packed[i], ("seq", "blk"), xor_pairs(seq_count, blk_count, *flips[i])
        )
    swap = [(0, 1), (1, 0)]
    other = [lax.ppermute(part, "chan", swap) for part in own]
    block = (seq_count, tokens, 128)
    kept, sent = pl.pallas_call(
        lambda *refs: attend_kernel(tokens, width, chips, seq_count, lat, blk_count, *refs),
        out_shape=[
            jax.ShapeDtypeStruct(block, jnp.float32),
            jax.ShapeDtypeStruct(block, jnp.bfloat16),
        ],
        in_specs=[vmem] * (2 * chips) + [hbm, vmem],
        out_specs=[vmem, vmem],
        scratch_shapes=[pltpu.VMEM((lat, width), jnp.bfloat16), pltpu.SemaphoreType.DMA],
        name="attend",
    )(*own, *other, head_weight.T, norm_gain.reshape(chips, width))
    arrived = lax.ppermute(sent, "blk", swap)
    near = (3, tokens, 128)
    outs = pl.pallas_call(
        lambda *refs: spread_kernel(lat, seq_count, *refs),
        out_shape=[jax.ShapeDtypeStruct(near, jnp.float32)]
        + [jax.ShapeDtypeStruct(near, jnp.bfloat16)] * (seq_count - 1),
        in_specs=[vmem, vmem],
        out_specs=[vmem] * seq_count,
        scratch_shapes=[pltpu.VMEM(block, jnp.float32)],
        name="spread",
    )(kept, arrived)
    moved = [
        lax.ppermute(outs[flip], "seq", [(s, s ^ flip) for s in range(seq_count)])
        for flip in range(1, seq_count)
    ]
    half = pl.pallas_call(
        lambda *refs: latent_kernel(lat, feat, seq_count, *refs),
        out_shape=jax.ShapeDtypeStruct((3, tokens, lat), jnp.bfloat16),
        in_specs=[vmem] * (seq_count + 1),
        out_specs=vmem,
        name="latent",
    )(outs[0], *moved, head_bias.reshape(1, lat))
    mate = lax.ppermute(half, "chan", swap)
    shape = (frame_dev, 3 * rows_dev, cols_dev, lat)
    half, mate = half.reshape(shape), mate.reshape(shape)
    first = lax.axis_index("chan") == 0
    wide_rows = jnp.concatenate(
        [jnp.where(first, half, mate), jnp.where(first, mate, half)], axis=2
    )
    return decode(wide_rows, rows_dev, in_weight, in_bias, conv_weight, conv_bias)


def per_device(queries, *rest):
    frame_dev, rows_dev, cols_dev, feat = queries.shape
    seq_count = lax.axis_size("seq")
    blk_count = lax.axis_size("blk")
    lat = rest[3].shape[1]
    fits = (
        frame_dev == 1
        and rows_dev == 2
        and (rows_dev * cols_dev) % 16 == 0
        and lat + 2 <= 128
        and blk_count == 2
        and seq_count & (seq_count - 1) == 0
        and lax.axis_size("chan") == 2
        and feat // HD % (seq_count * blk_count) == 0
    )
    return (exchanged if fits else gathered)(queries, *rest)


def solution(mesh):
    return jax.shard_map(
        per_device,
        mesh=mesh,
        in_specs=(
            P(("groups", "blk"), "seq", "chan", None),
            P(("groups", "blk"), "seq", "chan", None),
            P(("groups", "blk"), "seq", "chan", None),
            P(),
            P(),
            P(),
            P(),
            P(),
            P(None, None, None, "chan"),
            P("chan"),
        ),
        out_specs=P(("groups", "blk"), "seq", None, "chan"),
        check_vma=False,
    )
```

```python
import jax
import jax.numpy as jnp
from jax import lax
from jax.experimental import pallas as pl
from jax.experimental.pallas import tpu as pltpu
from jax.sharding import PartitionSpec as P

HD = 128


epsilon = 1e-06


def with_halo(cells, sides, width):
    for axis, dim in sides:
        count = lax.axis_size(axis)
        ends = count - 1
        head = lax.slice_in_dim(cells, 0, width, axis=dim)
        tail = lax.slice_in_dim(cells, cells.shape[dim] - width, cells.shape[dim], axis=dim)
        cells = jnp.concatenate(
            [
                lax.ppermute(tail, axis, [(i, (i + 1) % count) for i in range(ends)]),
                cells,
                lax.ppermute(head, axis, [((i + 1) % count, i) for i in range(ends)]),
            ],
            axis=dim,
        )
    return cells


def conv_valid(inputs, kernel):
    col_count = inputs.shape[2]
    padded = jnp.pad(inputs, ((0, 0), (0, 0), (1, 1), (0, 0)))
    stacked = jnp.concatenate(
        [padded[:, :, col_tap : col_tap + col_count, :] for col_tap in range(3)], axis=-1
    )
    rows_out = inputs.shape[1] - 2
    result = None
    for row_tap in range(3):
        flat_kernel = kernel[row_tap].reshape(3 * kernel.shape[2], kernel.shape[3])
        term = jnp.einsum(
            "frci,io->frco",
            stacked[:, row_tap : row_tap + rows_out],
            flat_kernel,
            preferred_element_type=jnp.float32,
        )
        result = term if result is None else result + term
    return result


def absorb(running, key_block, value_block, query_heads, score_scale):
    run_max, denoms, numers = running
    scores = (
        jnp.einsum("hqd,hkd->hqk", query_heads, key_block, preferred_element_type=jnp.float32)
        * score_scale
    )
    fresh_max = jnp.maximum(run_max, jnp.max(scores, axis=-1))
    rescale = jnp.exp(run_max - fresh_max)
    expo = jnp.exp(scores - fresh_max[..., None])
    denoms = denoms * rescale + jnp.sum(expo, axis=-1)
    numers = numers * rescale[..., None] + jnp.einsum(
        "hqk,hkd->hqd", expo.astype(jnp.bfloat16), value_block, preferred_element_type=jnp.float32
    )
    return (fresh_max, denoms, numers)


def decode(wide_rows, rows_dev, in_weight, in_bias, conv_weight, conv_bias):
    pre_act = conv_valid(wide_rows, in_weight) + in_bias
    row_ids = lax.axis_index("seq") * rows_dev - 1 + jnp.arange(rows_dev + 2, dtype=jnp.int32)
    inside = (row_ids >= 0) & (row_ids < rows_dev * lax.axis_size("seq"))
    activation = jnp.where(inside[None, :, None, None], jax.nn.silu(pre_act), 0.0).astype(
        jnp.bfloat16
    )
    return (conv_valid(activation, conv_weight) + conv_bias).astype(jnp.bfloat16)


def gathered(
    queries,
    keys,
    values,
    norm_gain,
    head_weight,
    head_bias,
    in_weight,
    in_bias,
    conv_weight,
    conv_bias,
):
    frame_dev, rows_dev, cols_dev, feat = queries.shape
    seq_count = lax.axis_size("seq")
    feat_dev = feat // seq_count
    heads_dev = feat_dev // HD
    score_scale = HD ** (-0.5)
    query_all, key_all, value_all = (
        lax.all_to_all(queries, "seq", split_axis=3, concat_axis=1, tiled=True),
        lax.all_to_all(keys, "seq", split_axis=3, concat_axis=1, tiled=True),
        lax.all_to_all(values, "seq", split_axis=3, concat_axis=1, tiled=True),
    )
    all_rows = query_all.shape[1]

    def to_heads(block):
        return block.reshape(-1, heads_dev, HD).transpose(1, 0, 2)

    query_heads = to_heads(query_all)
    key_heads = to_heads(key_all)
    value_heads = to_heads(value_all)
    token_local = query_heads.shape[1]

    def attend_piece(running, block_pair):
        key_piece, value_piece = block_pair
        key_rows = key_piece.shape[1]
        if key_rows > 1024 and key_rows % 1024 == 0:
            count = key_rows // 1024
            key_split = key_piece.reshape(heads_dev, count, 1024, HD).transpose(1, 0, 2, 3)
            value_split = value_piece.reshape(heads_dev, count, 1024, HD).transpose(1, 0, 2, 3)

            def step_block(state, pair_block):
                return (absorb(state, pair_block[0], pair_block[1], query_heads, score_scale), None)

            running, _ = lax.scan(step_block, running, (key_split, value_split))
            return running
        return absorb(running, key_piece, value_piece, query_heads, score_scale)

    start_state = (
        jnp.full((heads_dev, token_local), -1e30, jnp.float32),
        jnp.zeros((heads_dev, token_local), jnp.float32),
        jnp.zeros((heads_dev, token_local, HD), jnp.float32),
    )
    run_max, denoms, numers = attend_piece(
        start_state,
        (
            lax.all_gather(key_heads, ("blk", "chan"), axis=1, tiled=True),
            lax.all_gather(value_heads, ("blk", "chan"), axis=1, tiled=True),
        ),
    )
    attended = (numers / denoms[..., None]).astype(jnp.bfloat16)
    attended = attended.transpose(1, 0, 2).reshape(frame_dev, all_rows, cols_dev, feat_dev)
    back = lax.all_to_all(attended, "seq", split_axis=1, concat_axis=3, tiled=True)
    wide_att = back.astype(jnp.float32)
    squares = jnp.sum(wide_att * wide_att, axis=-1)
    normed = (wide_att * norm_gain).astype(jnp.bfloat16)
    projected = jnp.einsum("frcd,dl->frcl", normed, head_weight, preferred_element_type=jnp.float32)
    rms = jnp.sqrt(squares / feat + epsilon)
    latent_cols = (projected / rms[..., None] + head_bias).astype(jnp.bfloat16)
    latent = lax.all_gather(latent_cols, "chan", axis=2, tiled=True)
    wide_rows = with_halo(latent, (("seq", 1),), 2)
    return decode(wide_rows, rows_dev, in_weight, in_bias, conv_weight, conv_bias)


def xor_pairs(seq_count, blk_count, row_flip, blk_flip):
    return [
        (s * blk_count + b, (s ^ row_flip) * blk_count + (b ^ blk_flip))
        for s in range(seq_count)
        for b in range(blk_count)
    ]


def return_pairs(seq_count, flip):
    pairs = []
    for s in range(seq_count):
        for b in range(2):
            for core in range(2):
                if flip or core:
                    target = ((s ^ flip) * 2 + (b ^ core)) * 2 + core
                    pairs.append(((s * 2 + b) * 2 + core, target))
    return pairs


def pack_kernel(tokens, width, flips, blk_count, *refs):
    sources, head_t, gain = refs[:3], refs[3], refs[4]
    outs, weight, gains, sems = refs[5:-3], refs[-3], refs[-2], refs[-1]
    row = lax.axis_index("seq")
    blk = lax.axis_index("blk")
    copies = []
    for place, (row_flip, blk_flip) in enumerate(flips):
        target = (row ^ row_flip) * blk_count + (blk ^ blk_flip)
        start = pl.multiple_of(target * width, 128)
        for part, source in enumerate(sources):
            copies.append(
                (source.at[:, pl.ds(start, width)], outs[place].at[pl.ds(part * tokens, tokens), :])
            )
    start = pl.multiple_of((row * blk_count + blk) * width, 128)
    copies.append((head_t.at[:, pl.ds(start, width)], weight))
    copies.append((gain.at[:, pl.ds(start, width)], gains))
    copies = [
        pltpu.make_async_copy(source, out, sems.at[i]) for i, (source, out) in enumerate(copies)
    ]
    for copy in copies:
        copy.start()
    for copy in copies:
        copy.wait()


def stage_kernel(first, in_weight, weight, same, in_copy, copy, sems):
    del first, same
    moves = [
        pltpu.make_async_copy(source, out, sems.at[i])
        for i, (source, out) in enumerate(((in_weight, in_copy), (weight, copy)))
    ]
    for move in moves:
        move.start()
    for move in moves:
        move.wait()


def turn(block, shift):
    return pltpu.roll(block, shift % 128, 1) if shift % 128 else block


def pair_squares(total, lane):
    high = total.astype(jnp.bfloat16).astype(jnp.float32)
    rest = turn(total - high, 1)
    return jnp.where((lane == 0) | (lane == 2), high, jnp.where((lane == 1) | (lane == 3), rest, 0.0))


def attend_kernel(tokens, width, seq_count, lat, *refs):
    count = 2 * seq_count
    own = refs[:count]
    other = refs[count : 2 * count]
    weight, gains, kept = refs[2 * count : 2 * count + 3]
    sent, total, sums = refs[2 * count + 3 : -2], refs[-2], refs[-1]
    row = lax.axis_index("seq")
    first = lax.axis_index("chan") == 0
    factor = HD ** (-0.5) * 1.4426950408889634
    squares = None
    projected = None
    for head in range(width // HD):
        span = slice(head * HD, (head + 1) * HD)
        queries = []
        for near, far in zip(range(seq_count), range(seq_count, count)):
            queries.append(jnp.where(first, own[near][:tokens, span], other[far][:tokens, span]))
            queries.append(jnp.where(first, other[near][:tokens, span], own[far][:tokens, span]))
        query = jnp.concatenate(queries, axis=0)
        key = jnp.concatenate([ref[tokens : 2 * tokens, span] for ref in own + other], axis=0)
        value = jnp.concatenate([ref[2 * tokens :, span] for ref in own + other], axis=0)
        scores = lax.dot_general(
            query, key, (((1,), (1,)), ((), ())), preferred_element_type=jnp.float32
        )
        top = jnp.max(scores, axis=-1, keepdims=True)
        expo = jnp.exp2((scores - top) * factor)
        denom = jnp.sum(expo, axis=-1, keepdims=True)
        numer = jnp.dot(expo.astype(jnp.bfloat16), value, preferred_element_type=jnp.float32)
        attended = (numer / denom).astype(jnp.bfloat16).astype(jnp.float32)
        square = jnp.sum(attended * attended, axis=-1, keepdims=True)
        normed = (attended * gains[:, span]).astype(jnp.bfloat16)
        term = lax.dot_general(
            normed, weight[:, span], (((1,), (1,)), ((), ())), preferred_element_type=jnp.float32
        )
        squares = square if squares is None else squares + square
        projected = term if projected is None else projected + term
    half = tokens // 2
    lane = lax.broadcasted_iota(jnp.int32, (half, 128), 1)
    for place in range(seq_count):
        for side in range(2):
            start = (2 * place + side) * tokens
            middle, end = start + half, start + tokens
            total[place, side] = jnp.concatenate(
                [projected[start:middle], projected[middle:end]], axis=1
            )
            pair = jnp.where(
                lane == 0, squares[start:middle], jnp.where(lane == 2, squares[middle:end], 0.0)
            )
            sums[place, side] = pair_squares(pair, lane)
    for flip in range(seq_count):
        target = row ^ flip
        tail = None
        for step in range(3):
            source = target + step - 1
            valid = (source >= 0) & (source < seq_count)
            place = jnp.where(valid, source ^ row, 0)
            for side in range(2):
                piece = jnp.where(valid, total[place, side], 0.0)
                moved = turn(jnp.where(valid, sums[place, side], 0.0), 4 * (2 * step + side))
                tail = moved if tail is None else tail + moved
                sent[flip][2 * step + side] = piece.astype(jnp.bfloat16)
                if flip == 0:
                    kept[2 * step + side] = jnp.where(first, piece, 0.0)
        sent[flip][6] = tail.astype(jnp.bfloat16)
        if flip == 0:
            kept[6] = jnp.where(first, tail, 0.0)


def total_kernel(kept, *rest):
    arrived, out = rest[:-1], rest[-1]
    total = kept[...]
    for ref in arrived:
        total = total + ref[...].astype(jnp.float32)
    out[...] = total


def beside(cells, cols):
    count = cells.shape[0]
    col = lax.broadcasted_iota(jnp.int32, cells.shape, 0) % cols
    before = jnp.where(col == 0, 0.0, pltpu.roll(cells, 1, 0))
    after = jnp.where(col == cols - 1, 0.0, pltpu.roll(cells, count - 1, 0))
    return [part.astype(jnp.bfloat16) for part in (before, cells, after)]


def decode_kernel(
    lat, feat, cols_dev, seq_count, mine, mate, head_bias, in_weight, in_bias, weight, bias, out
):
    row = lax.axis_index("seq")
    cols = 2 * cols_dev
    sums = mine[6] + mate[6]
    lane = lax.broadcasted_iota(jnp.int32, sums.shape, 1)
    biases = jnp.concatenate([head_bias[...], head_bias[...]], axis=1)
    rows = []
    for step in range(3):
        sides = []
        for side in range(2):
            index = 2 * step + side
            upper, lower = (
                sums[:, 4 * index + at : 4 * index + at + 1]
                + sums[:, 4 * index + at + 1 : 4 * index + at + 2]
                for at in (0, 2)
            )
            rms = jnp.sqrt(jnp.where(lane < lat, upper, lower) / feat + epsilon)
            place = row + step - 1
            valid = (place >= 0) & (place < seq_count)
            latent = jnp.where(valid, (mine[index] + mate[index]) / rms + biases, 0.0)
            sides.append(latent.astype(jnp.bfloat16).astype(jnp.float32))
        rows += [side[:, :lat] for side in sides] + [side[:, lat:] for side in sides]
    wide = jnp.concatenate(beside(jnp.concatenate(rows, axis=0), cols), axis=1)
    deep = 3 * lat
    inner = 4 * cols
    pre = None
    for tap in range(3):
        term = jnp.dot(
            wide[tap * cols : tap * cols + inner],
            in_weight[tap * deep : (tap + 1) * deep, :],
            preferred_element_type=jnp.float32,
        )
        pre = term if pre is None else pre + term
    pre = pre + in_bias[...]
    active = pre / (1.0 + jnp.exp(-pre))
    place = 2 * row - 1 + lax.broadcasted_iota(jnp.int32, active.shape, 0) // cols
    active = jnp.where((place >= 0) & (place < 2 * seq_count), active, 0.0)
    active = active.astype(jnp.bfloat16).astype(jnp.float32)
    shifted = beside(active, cols)
    deep = active.shape[1]
    result = None
    for tap in range(3):
        for col_tap in range(3):
            start = (tap * 3 + col_tap) * deep
            term = jnp.dot(
                shifted[col_tap][tap * cols : (tap + 2) * cols],
                weight[start : start + deep, :],
                preferred_element_type=jnp.float32,
            )
            result = term if result is None else result + term
    out[...] = (result + bias[...]).astype(jnp.bfloat16)


def held(parts):
    return [pltpu.with_memory_space_constraint(part, pltpu.VMEM) for part in parts]


def parked(parts):
    return [pltpu.with_memory_space_constraint(part, pltpu.HBM) for part in parts]


def exchanged(
    queries,
    keys,
    values,
    norm_gain,
    head_weight,
    head_bias,
    in_weight,
    in_bias,
    conv_weight,
    conv_bias,
):
    frame_dev, rows_dev, cols_dev, feat = queries.shape
    seq_count = lax.axis_size("seq")
    blk_count = lax.axis_size("blk")
    lat = head_weight.shape[1]
    wide = in_weight.shape[3]
    out_dev = conv_weight.shape[3]
    tokens = frame_dev * rows_dev * cols_dev
    chips = seq_count * blk_count
    width = feat // chips
    flips = [(s, b) for b in range(blk_count) for s in range(seq_count)]
    vmem = pl.BlockSpec(memory_space=pltpu.VMEM)
    hbm = pl.BlockSpec(memory_space=pl.ANY)
    flat = [part.reshape(tokens, feat) for part in (queries, keys, values)]
    piece = pltpu.VMEM((3 * tokens, width), jnp.bfloat16)
    *packed, weight, gains = pl.pallas_call(
        lambda *refs: pack_kernel(tokens, width, flips, blk_count, *refs),
        out_shape=[piece] * chips
        + [pltpu.VMEM((lat, width), jnp.bfloat16), pltpu.VMEM((1, width), jnp.float32)],
        in_specs=[hbm] * 5,
        out_specs=[vmem] * (chips + 2),
        scratch_shapes=[pltpu.SemaphoreType.DMA((3 * chips + 2,))],
        compiler_params=pltpu.CompilerParams(vmem_limit_bytes=4 << 20),
        name="pack",
    )(*parked([*flat, head_weight.T, norm_gain.reshape(1, feat)]))
    order = sorted(range(1, chips), key=lambda i: (-(flips[i][0] >= seq_count // 2), i))
    own = [packed[0]] + [None] * (chips - 1)
    for i in order:
        own[i] = lax.ppermute(
            packed[i], ("seq", "blk"), xor_pairs(seq_count, blk_count, *flips[i])
        )
    own[0], in_held, conv_held = pl.pallas_call(
        stage_kernel,
        out_shape=[
            piece,
            pltpu.VMEM((9 * lat, wide), jnp.bfloat16),
            pltpu.VMEM((9 * wide, out_dev), jnp.bfloat16),
        ],
        in_specs=[hbm] * 3,
        out_specs=[hbm] * 3,
        input_output_aliases={0: 0},
        scratch_shapes=[pltpu.SemaphoreType.DMA((2,))],
        compiler_params=pltpu.CompilerParams(vmem_limit_bytes=4 << 20),
        name="stage",
    )(
        *held([own[0]]),
        *parked([in_weight.reshape(9 * lat, wide), conv_weight.reshape(9 * wide, out_dev)]),
    )
    swap = [(0, 1), (1, 0)]
    other = [lax.ppermute(part, "chan", swap) for part in own]
    shape = (7, tokens // 2, 128)
    block = pltpu.VMEM((seq_count, 2, tokens // 2, 128), jnp.float32)
    kept, *sent = pl.pallas_call(
        lambda *refs: attend_kernel(tokens, width, seq_count, lat, *refs),
        out_shape=[pltpu.VMEM(shape, jnp.float32)]
        + [pltpu.VMEM(shape, jnp.bfloat16)] * seq_count,
        in_specs=[vmem] * (2 * chips + 2),
        out_specs=[vmem] * (seq_count + 1),
        scratch_shapes=[block, block],
        compiler_params=pltpu.CompilerParams(vmem_limit_bytes=16 << 20),
        name="attend",
    )(*held(own + other + [weight, gains]))
    arrived = [
        lax.ppermute(part, ("seq", "blk", "chan"), return_pairs(seq_count, flip))
        for flip, part in enumerate(sent)
    ]
    mine = pl.pallas_call(
        total_kernel,
        out_shape=pltpu.VMEM(shape, jnp.float32),
        in_specs=[vmem] * (seq_count + 1),
        out_specs=vmem,
        compiler_params=pltpu.CompilerParams(vmem_limit_bytes=4 << 20),
        name="total",
    )(*held([kept, *arrived]))
    mate = lax.ppermute(mine, "chan", swap)
    decoded = pl.pallas_call(
        lambda *refs: decode_kernel(lat, feat, cols_dev, seq_count, *refs),
        out_shape=jax.ShapeDtypeStruct((2 * tokens, out_dev), jnp.bfloat16),
        in_specs=[vmem] * 7,
        out_specs=vmem,
        compiler_params=pltpu.CompilerParams(vmem_limit_bytes=16 << 20),
        name="decode",
    )(
        *held(
            [
                mine,
                mate,
                head_bias.reshape(1, lat),
                in_held,
                in_bias.reshape(1, wide),
                conv_held,
                conv_bias.reshape(1, out_dev),
            ]
        )
    )
    return decoded.reshape(frame_dev, rows_dev, 2 * cols_dev, out_dev)


def per_device(queries, *rest):
    frame_dev, rows_dev, cols_dev, feat = queries.shape
    seq_count = lax.axis_size("seq")
    blk_count = lax.axis_size("blk")
    lat = rest[3].shape[1]
    fits = (
        frame_dev == 1
        and rows_dev == 2
        and cols_dev % 16 == 0
        and lat == 64
        and blk_count == 2
        and seq_count & (seq_count - 1) == 0
        and lax.axis_size("chan") == 2
        and feat // HD % (seq_count * blk_count) == 0
    )
    return (exchanged if fits else gathered)(queries, *rest)


def solution(mesh):
    return jax.shard_map(
        per_device,
        mesh=mesh,
        in_specs=(
            P(("groups", "blk"), "seq", "chan", None),
            P(("groups", "blk"), "seq", "chan", None),
            P(("groups", "blk"), "seq", "chan", None),
            P(),
            P(),
            P(),
            P(),
            P(),
            P(None, None, None, "chan"),
            P("chan"),
        ),
        out_specs=P(("groups", "blk"), "seq", None, "chan"),
        check_vma=False,
    )
```

```python
import jax
import jax.numpy as jnp
from jax import lax
from jax.experimental import pallas as pl
from jax.experimental.pallas import tpu as pltpu
from jax.sharding import PartitionSpec as P

HD = 128


epsilon = 1e-06


def with_halo(cells, sides, width):
    for axis, dim in sides:
        count = lax.axis_size(axis)
        ends = count - 1
        head = lax.slice_in_dim(cells, 0, width, axis=dim)
        tail = lax.slice_in_dim(cells, cells.shape[dim] - width, cells.shape[dim], axis=dim)
        cells = jnp.concatenate(
            [
                lax.ppermute(tail, axis, [(i, (i + 1) % count) for i in range(ends)]),
                cells,
                lax.ppermute(head, axis, [((i + 1) % count, i) for i in range(ends)]),
            ],
            axis=dim,
        )
    return cells


def conv_valid(inputs, kernel):
    col_count = inputs.shape[2]
    padded = jnp.pad(inputs, ((0, 0), (0, 0), (1, 1), (0, 0)))
    stacked = jnp.concatenate(
        [padded[:, :, col_tap : col_tap + col_count, :] for col_tap in range(3)], axis=-1
    )
    rows_out = inputs.shape[1] - 2
    result = None
    for row_tap in range(3):
        flat_kernel = kernel[row_tap].reshape(3 * kernel.shape[2], kernel.shape[3])
        term = jnp.einsum(
            "frci,io->frco",
            stacked[:, row_tap : row_tap + rows_out],
            flat_kernel,
            preferred_element_type=jnp.float32,
        )
        result = term if result is None else result + term
    return result


def absorb(running, key_block, value_block, query_heads, score_scale):
    run_max, denoms, numers = running
    scores = (
        jnp.einsum("hqd,hkd->hqk", query_heads, key_block, preferred_element_type=jnp.float32)
        * score_scale
    )
    fresh_max = jnp.maximum(run_max, jnp.max(scores, axis=-1))
    rescale = jnp.exp(run_max - fresh_max)
    expo = jnp.exp(scores - fresh_max[..., None])
    denoms = denoms * rescale + jnp.sum(expo, axis=-1)
    numers = numers * rescale[..., None] + jnp.einsum(
        "hqk,hkd->hqd", expo.astype(jnp.bfloat16), value_block, preferred_element_type=jnp.float32
    )
    return (fresh_max, denoms, numers)


def decode(wide_rows, rows_dev, in_weight, in_bias, conv_weight, conv_bias):
    pre_act = conv_valid(wide_rows, in_weight) + in_bias
    row_ids = lax.axis_index("seq") * rows_dev - 1 + jnp.arange(rows_dev + 2, dtype=jnp.int32)
    inside = (row_ids >= 0) & (row_ids < rows_dev * lax.axis_size("seq"))
    activation = jnp.where(inside[None, :, None, None], jax.nn.silu(pre_act), 0.0).astype(
        jnp.bfloat16
    )
    return (conv_valid(activation, conv_weight) + conv_bias).astype(jnp.bfloat16)


def gathered(
    queries,
    keys,
    values,
    norm_gain,
    head_weight,
    head_bias,
    in_weight,
    in_bias,
    conv_weight,
    conv_bias,
):
    frame_dev, rows_dev, cols_dev, feat = queries.shape
    seq_count = lax.axis_size("seq")
    feat_dev = feat // seq_count
    heads_dev = feat_dev // HD
    score_scale = HD ** (-0.5)
    query_all, key_all, value_all = (
        lax.all_to_all(queries, "seq", split_axis=3, concat_axis=1, tiled=True),
        lax.all_to_all(keys, "seq", split_axis=3, concat_axis=1, tiled=True),
        lax.all_to_all(values, "seq", split_axis=3, concat_axis=1, tiled=True),
    )
    all_rows = query_all.shape[1]

    def to_heads(block):
        return block.reshape(-1, heads_dev, HD).transpose(1, 0, 2)

    query_heads = to_heads(query_all)
    key_heads = to_heads(key_all)
    value_heads = to_heads(value_all)
    token_local = query_heads.shape[1]

    def attend_piece(running, block_pair):
        key_piece, value_piece = block_pair
        key_rows = key_piece.shape[1]
        if key_rows > 1024 and key_rows % 1024 == 0:
            count = key_rows // 1024
            key_split = key_piece.reshape(heads_dev, count, 1024, HD).transpose(1, 0, 2, 3)
            value_split = value_piece.reshape(heads_dev, count, 1024, HD).transpose(1, 0, 2, 3)

            def step_block(state, pair_block):
                return (absorb(state, pair_block[0], pair_block[1], query_heads, score_scale), None)

            running, _ = lax.scan(step_block, running, (key_split, value_split))
            return running
        return absorb(running, key_piece, value_piece, query_heads, score_scale)

    start_state = (
        jnp.full((heads_dev, token_local), -1e30, jnp.float32),
        jnp.zeros((heads_dev, token_local), jnp.float32),
        jnp.zeros((heads_dev, token_local, HD), jnp.float32),
    )
    run_max, denoms, numers = attend_piece(
        start_state,
        (
            lax.all_gather(key_heads, ("blk", "chan"), axis=1, tiled=True),
            lax.all_gather(value_heads, ("blk", "chan"), axis=1, tiled=True),
        ),
    )
    attended = (numers / denoms[..., None]).astype(jnp.bfloat16)
    attended = attended.transpose(1, 0, 2).reshape(frame_dev, all_rows, cols_dev, feat_dev)
    back = lax.all_to_all(attended, "seq", split_axis=1, concat_axis=3, tiled=True)
    wide_att = back.astype(jnp.float32)
    squares = jnp.sum(wide_att * wide_att, axis=-1)
    normed = (wide_att * norm_gain).astype(jnp.bfloat16)
    projected = jnp.einsum("frcd,dl->frcl", normed, head_weight, preferred_element_type=jnp.float32)
    rms = jnp.sqrt(squares / feat + epsilon)
    latent_cols = (projected / rms[..., None] + head_bias).astype(jnp.bfloat16)
    latent = lax.all_gather(latent_cols, "chan", axis=2, tiled=True)
    wide_rows = with_halo(latent, (("seq", 1),), 2)
    return decode(wide_rows, rows_dev, in_weight, in_bias, conv_weight, conv_bias)


def xor_pairs(seq_count, blk_count, row_flip, blk_flip):
    return [
        (s * blk_count + b, (s ^ row_flip) * blk_count + (b ^ blk_flip))
        for s in range(seq_count)
        for b in range(blk_count)
    ]


def start_rank(seq_count):
    def rank(flip):
        row_flip, blk_flip = flip
        crossing = row_flip >= seq_count // 2
        late = 2 if crossing and blk_flip else (0 if crossing else 1)
        return (flip != (0, 0), late, row_flip, blk_flip)

    return rank


def return_pairs(seq_count, flip):
    pairs = []
    for s in range(seq_count):
        for b in range(2):
            for core in range(2):
                if flip or core:
                    target = ((s ^ flip) * 2 + (b ^ core)) * 2 + core
                    pairs.append(((s * 2 + b) * 2 + core, target))
    return pairs


def pack_kernel(tokens, width, flips, blk_count, *refs):
    sources, head_t, gain = refs[:3], refs[3], refs[4]
    outs, weight, gains, sems = refs[5:-3], refs[-3], refs[-2], refs[-1]
    row = lax.axis_index("seq")
    blk = lax.axis_index("blk")
    copies = []
    for place, (row_flip, blk_flip) in enumerate(flips):
        target = (row ^ row_flip) * blk_count + (blk ^ blk_flip)
        start = pl.multiple_of(target * width, 128)
        for part, source in enumerate(sources):
            copies.append(
                (source.at[:, pl.ds(start, width)], outs[place].at[pl.ds(part * tokens, tokens), :])
            )
    start = pl.multiple_of((row * blk_count + blk) * width, 128)
    copies.append((head_t.at[:, pl.ds(start, width)], weight))
    copies.append((gain.at[:, pl.ds(start, width)], gains))
    copies = [
        pltpu.make_async_copy(source, out, sems.at[i]) for i, (source, out) in enumerate(copies)
    ]
    for copy in copies:
        copy.start()
    for copy in copies:
        copy.wait()


def stage_kernel(first, in_weight, weight, same, in_copy, copy, sems):
    del first, same
    moves = [
        pltpu.make_async_copy(source, out, sems.at[i])
        for i, (source, out) in enumerate(((in_weight, in_copy), (weight, copy)))
    ]
    for move in moves:
        move.start()
    for move in moves:
        move.wait()


def turn(block, shift):
    return pltpu.roll(block, shift % 128, 1) if shift % 128 else block


def pair_squares(total, lane):
    high = total.astype(jnp.bfloat16).astype(jnp.float32)
    rest = turn(total - high, 1)
    return jnp.where((lane == 0) | (lane == 2), high, jnp.where((lane == 1) | (lane == 3), rest, 0.0))


def attend_kernel(tokens, width, seq_count, lat, seat, *refs):
    count = 2 * seq_count
    own = [refs[i] for i in seat]
    other = [refs[count + i] for i in seat]
    weight, gains, kept = refs[2 * count : 2 * count + 3]
    sent, total, sums = refs[2 * count + 3 : -2], refs[-2], refs[-1]
    row = lax.axis_index("seq")
    first = lax.axis_index("chan") == 0
    factor = HD ** (-0.5) * 1.4426950408889634
    squares = None
    projected = None
    for head in range(width // HD):
        span = slice(head * HD, (head + 1) * HD)
        queries = []
        for near, far in zip(range(seq_count), range(seq_count, count)):
            queries.append(jnp.where(first, own[near][:tokens, span], other[far][:tokens, span]))
            queries.append(jnp.where(first, other[near][:tokens, span], own[far][:tokens, span]))
        query = jnp.concatenate(queries, axis=0)
        key = jnp.concatenate([ref[tokens : 2 * tokens, span] for ref in own + other], axis=0)
        value = jnp.concatenate([ref[2 * tokens :, span] for ref in own + other], axis=0)
        scores = lax.dot_general(
            query, key, (((1,), (1,)), ((), ())), preferred_element_type=jnp.float32
        )
        top = jnp.max(scores, axis=-1, keepdims=True)
        expo = jnp.exp2((scores - top) * factor)
        denom = jnp.sum(expo, axis=-1, keepdims=True)
        numer = jnp.dot(expo.astype(jnp.bfloat16), value, preferred_element_type=jnp.float32)
        attended = (numer / denom).astype(jnp.bfloat16).astype(jnp.float32)
        square = jnp.sum(attended * attended, axis=-1, keepdims=True)
        normed = (attended * gains[:, span]).astype(jnp.bfloat16)
        term = lax.dot_general(
            normed, weight[:, span], (((1,), (1,)), ((), ())), preferred_element_type=jnp.float32
        )
        squares = square if squares is None else squares + square
        projected = term if projected is None else projected + term
    half = tokens // 2
    lane = lax.broadcasted_iota(jnp.int32, (half, 128), 1)
    for place in range(seq_count):
        for side in range(2):
            start = (2 * place + side) * tokens
            middle, end = start + half, start + tokens
            total[place, side] = jnp.concatenate(
                [projected[start:middle], projected[middle:end]], axis=1
            )
            pair = jnp.where(
                lane == 0, squares[start:middle], jnp.where(lane == 2, squares[middle:end], 0.0)
            )
            sums[place, side] = pair_squares(pair, lane)
    for flip in range(seq_count):
        target = row ^ flip
        tail = None
        for step in range(3):
            source = target + step - 1
            valid = (source >= 0) & (source < seq_count)
            place = jnp.where(valid, source ^ row, 0)
            for side in range(2):
                piece = jnp.where(valid, total[place, side], 0.0)
                moved = turn(jnp.where(valid, sums[place, side], 0.0), 4 * (2 * step + side))
                tail = moved if tail is None else tail + moved
                sent[flip][2 * step + side] = piece.astype(jnp.bfloat16)
                if flip == 0:
                    kept[2 * step + side] = jnp.where(first, piece, 0.0)
        sent[flip][6] = tail.astype(jnp.bfloat16)
        if flip == 0:
            kept[6] = jnp.where(first, tail, 0.0)


def total_kernel(kept, *rest):
    arrived, out = rest[:-1], rest[-1]
    total = kept[...]
    for ref in arrived:
        total = total + ref[...].astype(jnp.float32)
    out[...] = total


def beside(cells, cols):
    count = cells.shape[0]
    col = lax.broadcasted_iota(jnp.int32, cells.shape, 0) % cols
    before = jnp.where(col == 0, 0.0, pltpu.roll(cells, 1, 0))
    after = jnp.where(col == cols - 1, 0.0, pltpu.roll(cells, count - 1, 0))
    return [part.astype(jnp.bfloat16) for part in (before, cells, after)]


def decode_kernel(
    lat, feat, cols_dev, seq_count, mine, mate, head_bias, in_weight, in_bias, weight, bias, out
):
    row = lax.axis_index("seq")
    cols = 2 * cols_dev
    sums = mine[6] + mate[6]
    lane = lax.broadcasted_iota(jnp.int32, sums.shape, 1)
    biases = jnp.concatenate([head_bias[...], head_bias[...]], axis=1)
    rows = []
    for step in range(3):
        sides = []
        for side in range(2):
            index = 2 * step + side
            upper, lower = (
                sums[:, 4 * index + at : 4 * index + at + 1]
                + sums[:, 4 * index + at + 1 : 4 * index + at + 2]
                for at in (0, 2)
            )
            rms = jnp.sqrt(jnp.where(lane < lat, upper, lower) / feat + epsilon)
            place = row + step - 1
            valid = (place >= 0) & (place < seq_count)
            latent = jnp.where(valid, (mine[index] + mate[index]) / rms + biases, 0.0)
            sides.append(latent.astype(jnp.bfloat16).astype(jnp.float32))
        rows += [side[:, :lat] for side in sides] + [side[:, lat:] for side in sides]
    wide = jnp.concatenate(beside(jnp.concatenate(rows, axis=0), cols), axis=1)
    deep = 3 * lat
    inner = 4 * cols
    pre = None
    for tap in range(3):
        term = jnp.dot(
            wide[tap * cols : tap * cols + inner],
            in_weight[tap * deep : (tap + 1) * deep, :],
            preferred_element_type=jnp.float32,
        )
        pre = term if pre is None else pre + term
    pre = pre + in_bias[...]
    active = pre / (1.0 + jnp.exp(-pre))
    place = 2 * row - 1 + lax.broadcasted_iota(jnp.int32, active.shape, 0) // cols
    active = jnp.where((place >= 0) & (place < 2 * seq_count), active, 0.0)
    active = active.astype(jnp.bfloat16).astype(jnp.float32)
    shifted = beside(active, cols)
    deep = active.shape[1]
    result = None
    for tap in range(3):
        for col_tap in range(3):
            start = (tap * 3 + col_tap) * deep
            term = jnp.dot(
                shifted[col_tap][tap * cols : (tap + 2) * cols],
                weight[start : start + deep, :],
                preferred_element_type=jnp.float32,
            )
            result = term if result is None else result + term
    out[...] = (result + bias[...]).astype(jnp.bfloat16)


def held(parts):
    return [pltpu.with_memory_space_constraint(part, pltpu.VMEM) for part in parts]


def parked(parts):
    return [pltpu.with_memory_space_constraint(part, pltpu.HBM) for part in parts]


def exchanged(
    queries,
    keys,
    values,
    norm_gain,
    head_weight,
    head_bias,
    in_weight,
    in_bias,
    conv_weight,
    conv_bias,
):
    frame_dev, rows_dev, cols_dev, feat = queries.shape
    seq_count = lax.axis_size("seq")
    blk_count = lax.axis_size("blk")
    lat = head_weight.shape[1]
    wide = in_weight.shape[3]
    out_dev = conv_weight.shape[3]
    tokens = frame_dev * rows_dev * cols_dev
    chips = seq_count * blk_count
    width = feat // chips
    near = [(s, b) for b in range(blk_count) for s in range(seq_count)]
    flips = sorted(near, key=start_rank(seq_count))
    vmem = pl.BlockSpec(memory_space=pltpu.VMEM)
    hbm = pl.BlockSpec(memory_space=pl.ANY)
    flat = [part.reshape(tokens, feat) for part in (queries, keys, values)]
    piece = pltpu.VMEM((3 * tokens, width), jnp.bfloat16)
    *packed, weight, gains = pl.pallas_call(
        lambda *refs: pack_kernel(tokens, width, flips, blk_count, *refs),
        out_shape=[piece] * chips
        + [pltpu.VMEM((lat, width), jnp.bfloat16), pltpu.VMEM((1, width), jnp.float32)],
        in_specs=[hbm] * 5,
        out_specs=[vmem] * (chips + 2),
        scratch_shapes=[pltpu.SemaphoreType.DMA((3 * chips + 2,))],
        compiler_params=pltpu.CompilerParams(vmem_limit_bytes=4 << 20),
        name="pack",
    )(*parked([*flat, head_weight.T, norm_gain.reshape(1, feat)]))
    own = [packed[0]] + [None] * (chips - 1)
    for i in range(1, chips):
        own[i] = lax.ppermute(
            packed[i], ("seq", "blk"), xor_pairs(seq_count, blk_count, *flips[i])
        )
    own[0], in_held, conv_held = pl.pallas_call(
        stage_kernel,
        out_shape=[
            piece,
            pltpu.VMEM((9 * lat, wide), jnp.bfloat16),
            pltpu.VMEM((9 * wide, out_dev), jnp.bfloat16),
        ],
        in_specs=[hbm] * 3,
        out_specs=[hbm] * 3,
        input_output_aliases={0: 0},
        scratch_shapes=[pltpu.SemaphoreType.DMA((2,))],
        compiler_params=pltpu.CompilerParams(vmem_limit_bytes=4 << 20),
        name="stage",
    )(
        *held([own[0]]),
        *parked([in_weight.reshape(9 * lat, wide), conv_weight.reshape(9 * wide, out_dev)]),
    )
    swap = [(0, 1), (1, 0)]
    other = [lax.ppermute(part, "chan", swap) for part in own]
    seat = [flips.index(flip) for flip in near]
    shape = (7, tokens // 2, 128)
    block = pltpu.VMEM((seq_count, 2, tokens // 2, 128), jnp.float32)
    kept, *sent = pl.pallas_call(
        lambda *refs: attend_kernel(tokens, width, seq_count, lat, seat, *refs),
        out_shape=[pltpu.VMEM(shape, jnp.float32)]
        + [pltpu.VMEM(shape, jnp.bfloat16)] * seq_count,
        in_specs=[vmem] * (2 * chips + 2),
        out_specs=[vmem] * (seq_count + 1),
        scratch_shapes=[block, block],
        compiler_params=pltpu.CompilerParams(vmem_limit_bytes=16 << 20),
        name="attend",
    )(*held(own + other + [weight, gains]))
    arrived = [
        lax.ppermute(sent[flip], ("seq", "blk", "chan"), return_pairs(seq_count, flip))
        for flip in reversed(range(seq_count))
    ]
    mine = pl.pallas_call(
        total_kernel,
        out_shape=pltpu.VMEM(shape, jnp.float32),
        in_specs=[vmem] * (seq_count + 1),
        out_specs=vmem,
        compiler_params=pltpu.CompilerParams(vmem_limit_bytes=4 << 20),
        name="total",
    )(*held([kept, *arrived]))
    mate = lax.ppermute(mine, "chan", swap)
    decoded = pl.pallas_call(
        lambda *refs: decode_kernel(lat, feat, cols_dev, seq_count, *refs),
        out_shape=jax.ShapeDtypeStruct((2 * tokens, out_dev), jnp.bfloat16),
        in_specs=[vmem] * 7,
        out_specs=vmem,
        compiler_params=pltpu.CompilerParams(vmem_limit_bytes=16 << 20),
        name="decode",
    )(
        *held(
            [
                mine,
                mate,
                head_bias.reshape(1, lat),
                in_held,
                in_bias.reshape(1, wide),
                conv_held,
                conv_bias.reshape(1, out_dev),
            ]
        )
    )
    return decoded.reshape(frame_dev, rows_dev, 2 * cols_dev, out_dev)


def per_device(queries, *rest):
    frame_dev, rows_dev, cols_dev, feat = queries.shape
    seq_count = lax.axis_size("seq")
    blk_count = lax.axis_size("blk")
    lat = rest[3].shape[1]
    fits = (
        frame_dev == 1
        and rows_dev == 2
        and cols_dev % 16 == 0
        and lat == 64
        and blk_count == 2
        and seq_count & (seq_count - 1) == 0
        and lax.axis_size("chan") == 2
        and feat // HD % (seq_count * blk_count) == 0
    )
    return (exchanged if fits else gathered)(queries, *rest)


def solution(mesh):
    return jax.shard_map(
        per_device,
        mesh=mesh,
        in_specs=(
            P(("groups", "blk"), "seq", "chan", None),
            P(("groups", "blk"), "seq", "chan", None),
            P(("groups", "blk"), "seq", "chan", None),
            P(),
            P(),
            P(),
            P(),
            P(),
            P(None, None, None, "chan"),
            P("chan"),
        ),
        out_specs=P(("groups", "blk"), "seq", None, "chan"),
        check_vma=False,
    )
```

```python
import jax
import jax.numpy as jnp
from jax import lax
from jax.experimental import pallas as pl
from jax.experimental.pallas import tpu as pltpu
from jax.sharding import PartitionSpec as P

HD = 128


epsilon = 1e-06


def with_halo(cells, sides, width):
    for axis, dim in sides:
        count = lax.axis_size(axis)
        ends = count - 1
        head = lax.slice_in_dim(cells, 0, width, axis=dim)
        tail = lax.slice_in_dim(cells, cells.shape[dim] - width, cells.shape[dim], axis=dim)
        cells = jnp.concatenate(
            [
                lax.ppermute(tail, axis, [(i, (i + 1) % count) for i in range(ends)]),
                cells,
                lax.ppermute(head, axis, [((i + 1) % count, i) for i in range(ends)]),
            ],
            axis=dim,
        )
    return cells


def conv_valid(inputs, kernel):
    col_count = inputs.shape[2]
    padded = jnp.pad(inputs, ((0, 0), (0, 0), (1, 1), (0, 0)))
    stacked = jnp.concatenate(
        [padded[:, :, col_tap : col_tap + col_count, :] for col_tap in range(3)], axis=-1
    )
    rows_out = inputs.shape[1] - 2
    result = None
    for row_tap in range(3):
        flat_kernel = kernel[row_tap].reshape(3 * kernel.shape[2], kernel.shape[3])
        term = jnp.einsum(
            "frci,io->frco",
            stacked[:, row_tap : row_tap + rows_out],
            flat_kernel,
            preferred_element_type=jnp.float32,
        )
        result = term if result is None else result + term
    return result


def absorb(running, key_block, value_block, query_heads, score_scale):
    run_max, denoms, numers = running
    scores = (
        jnp.einsum("hqd,hkd->hqk", query_heads, key_block, preferred_element_type=jnp.float32)
        * score_scale
    )
    fresh_max = jnp.maximum(run_max, jnp.max(scores, axis=-1))
    rescale = jnp.exp(run_max - fresh_max)
    expo = jnp.exp(scores - fresh_max[..., None])
    denoms = denoms * rescale + jnp.sum(expo, axis=-1)
    numers = numers * rescale[..., None] + jnp.einsum(
        "hqk,hkd->hqd", expo.astype(jnp.bfloat16), value_block, preferred_element_type=jnp.float32
    )
    return (fresh_max, denoms, numers)


def decode(wide_rows, rows_dev, in_weight, in_bias, conv_weight, conv_bias):
    pre_act = conv_valid(wide_rows, in_weight) + in_bias
    row_ids = lax.axis_index("seq") * rows_dev - 1 + jnp.arange(rows_dev + 2, dtype=jnp.int32)
    inside = (row_ids >= 0) & (row_ids < rows_dev * lax.axis_size("seq"))
    activation = jnp.where(inside[None, :, None, None], jax.nn.silu(pre_act), 0.0).astype(
        jnp.bfloat16
    )
    return (conv_valid(activation, conv_weight) + conv_bias).astype(jnp.bfloat16)


def gathered(
    queries,
    keys,
    values,
    norm_gain,
    head_weight,
    head_bias,
    in_weight,
    in_bias,
    conv_weight,
    conv_bias,
):
    frame_dev, rows_dev, cols_dev, feat = queries.shape
    seq_count = lax.axis_size("seq")
    feat_dev = feat // seq_count
    heads_dev = feat_dev // HD
    score_scale = HD ** (-0.5)
    query_all, key_all, value_all = (
        lax.all_to_all(queries, "seq", split_axis=3, concat_axis=1, tiled=True),
        lax.all_to_all(keys, "seq", split_axis=3, concat_axis=1, tiled=True),
        lax.all_to_all(values, "seq", split_axis=3, concat_axis=1, tiled=True),
    )
    all_rows = query_all.shape[1]

    def to_heads(block):
        return block.reshape(-1, heads_dev, HD).transpose(1, 0, 2)

    query_heads = to_heads(query_all)
    key_heads = to_heads(key_all)
    value_heads = to_heads(value_all)
    token_local = query_heads.shape[1]

    def attend_piece(running, block_pair):
        key_piece, value_piece = block_pair
        key_rows = key_piece.shape[1]
        if key_rows > 1024 and key_rows % 1024 == 0:
            count = key_rows // 1024
            key_split = key_piece.reshape(heads_dev, count, 1024, HD).transpose(1, 0, 2, 3)
            value_split = value_piece.reshape(heads_dev, count, 1024, HD).transpose(1, 0, 2, 3)

            def step_block(state, pair_block):
                return (absorb(state, pair_block[0], pair_block[1], query_heads, score_scale), None)

            running, _ = lax.scan(step_block, running, (key_split, value_split))
            return running
        return absorb(running, key_piece, value_piece, query_heads, score_scale)

    start_state = (
        jnp.full((heads_dev, token_local), -1e30, jnp.float32),
        jnp.zeros((heads_dev, token_local), jnp.float32),
        jnp.zeros((heads_dev, token_local, HD), jnp.float32),
    )
    run_max, denoms, numers = attend_piece(
        start_state,
        (
            lax.all_gather(key_heads, ("blk", "chan"), axis=1, tiled=True),
            lax.all_gather(value_heads, ("blk", "chan"), axis=1, tiled=True),
        ),
    )
    attended = (numers / denoms[..., None]).astype(jnp.bfloat16)
    attended = attended.transpose(1, 0, 2).reshape(frame_dev, all_rows, cols_dev, feat_dev)
    back = lax.all_to_all(attended, "seq", split_axis=1, concat_axis=3, tiled=True)
    wide_att = back.astype(jnp.float32)
    squares = jnp.sum(wide_att * wide_att, axis=-1)
    normed = (wide_att * norm_gain).astype(jnp.bfloat16)
    projected = jnp.einsum("frcd,dl->frcl", normed, head_weight, preferred_element_type=jnp.float32)
    rms = jnp.sqrt(squares / feat + epsilon)
    latent_cols = (projected / rms[..., None] + head_bias).astype(jnp.bfloat16)
    latent = lax.all_gather(latent_cols, "chan", axis=2, tiled=True)
    wide_rows = with_halo(latent, (("seq", 1),), 2)
    return decode(wide_rows, rows_dev, in_weight, in_bias, conv_weight, conv_bias)


def xor_pairs(seq_count, blk_count, row_flip, blk_flip):
    return [
        (s * blk_count + b, (s ^ row_flip) * blk_count + (b ^ blk_flip))
        for s in range(seq_count)
        for b in range(blk_count)
    ]


def start_rank(seq_count):
    def rank(flip):
        row_flip, blk_flip = flip
        far = row_flip > seq_count // 2
        late = 2 if far else (0 if row_flip == seq_count // 2 else 1)
        return (flip != (0, 0), late, -row_flip, -blk_flip if far else blk_flip)

    return rank


def return_pairs(seq_count, flip):
    pairs = []
    for s in range(seq_count):
        for b in range(2):
            for core in range(2):
                if flip or core:
                    target = ((s ^ flip) * 2 + (b ^ core)) * 2 + core
                    pairs.append(((s * 2 + b) * 2 + core, target))
    return pairs


def pack_kernel(tokens, width, flips, blk_count, *refs):
    sources, head_t, gain = refs[:3], refs[3], refs[4]
    outs, weight, gains, whole, sems = refs[5:-4], refs[-4], refs[-3], refs[-2], refs[-1]
    row = lax.axis_index("seq")
    blk = lax.axis_index("blk")
    start = pl.multiple_of((row * blk_count + blk) * width, 128)
    copies = [(source, whole.at[part]) for part, source in enumerate(sources)]
    copies.append((head_t.at[:, pl.ds(start, width)], weight))
    copies.append((gain.at[:, pl.ds(start, width)], gains))
    copies = [
        pltpu.make_async_copy(source, out, sems.at[i]) for i, (source, out) in enumerate(copies)
    ]
    for copy in copies:
        copy.start()
    for part, copy in enumerate(copies):
        copy.wait()
        if part < 3:
            for place, (row_flip, blk_flip) in enumerate(flips):
                target = (row ^ row_flip) * blk_count + (blk ^ blk_flip)
                begin = pl.multiple_of(target * width, 128)
                outs[place][part * tokens : (part + 1) * tokens, :] = whole[
                    part, :, pl.ds(begin, width)
                ]


def stage_kernel(first, in_weight, weight, same, in_copy, copy, sems):
    del first, same
    moves = [
        pltpu.make_async_copy(source, out, sems.at[i])
        for i, (source, out) in enumerate(((in_weight, in_copy), (weight, copy)))
    ]
    for move in moves:
        move.start()
    for move in moves:
        move.wait()


def attend_kernel(tokens, width, seq_count, lat, seat, *refs):
    count = 2 * seq_count
    own = [refs[i] for i in seat]
    other = [refs[count + i] for i in seat]
    weight, gains, kept = refs[2 * count : 2 * count + 3]
    sent, total = refs[2 * count + 3 : -1], refs[-1]
    row = lax.axis_index("seq")
    first = lax.axis_index("chan") == 0
    factor = HD ** (-0.5) * 1.4426950408889634
    spans = [slice(head * HD, (head + 1) * HD) for head in range(width // HD)]
    scores = []
    for span in spans:
        queries = []
        for near, far in zip(range(seq_count), range(seq_count, count)):
            queries.append(jnp.where(first, own[near][:tokens, span], other[far][:tokens, span]))
            queries.append(jnp.where(first, other[near][:tokens, span], own[far][:tokens, span]))
        query = jnp.concatenate(queries, axis=0)
        key = jnp.concatenate([ref[tokens : 2 * tokens, span] for ref in own + other], axis=0)
        scores.append(
            lax.dot_general(
                query, key, (((1,), (1,)), ((), ())), preferred_element_type=jnp.float32
            )
        )
    tops = [jnp.max(score, axis=-1, keepdims=True) for score in scores]
    expos = [jnp.exp2((score - top) * factor) for score, top in zip(scores, tops)]
    denoms = [jnp.sum(expo, axis=-1, keepdims=True) for expo in expos]
    numers = [
        jnp.dot(
            expo.astype(jnp.bfloat16),
            jnp.concatenate([ref[2 * tokens :, span] for ref in own + other], axis=0),
            preferred_element_type=jnp.float32,
        )
        for expo, span in zip(expos, spans)
    ]
    attended = [
        (numer / denom).astype(jnp.bfloat16).astype(jnp.float32)
        for numer, denom in zip(numers, denoms)
    ]
    squares = sum(part * part for part in attended)
    normed = jnp.concatenate(
        [(part * gains[:, span]).astype(jnp.bfloat16) for part, span in zip(attended, spans)],
        axis=1,
    )
    projected = lax.dot_general(
        normed, weight[...], (((1,), (1,)), ((), ())), preferred_element_type=jnp.float32
    )
    half = tokens // 2
    lane = lax.broadcasted_iota(jnp.int32, (half, 128), 1)
    squares = jnp.broadcast_to(jnp.sum(squares, axis=-1, keepdims=True), squares.shape)
    high = squares.astype(jnp.bfloat16).astype(jnp.float32)
    low = squares - high
    tail = jnp.zeros((half, 128), jnp.float32)
    for place in range(seq_count):
        for side in range(2):
            start = (2 * place + side) * tokens
            middle, end = start + half, start + tokens
            total[place, side] = jnp.concatenate(
                [projected[start:middle], projected[middle:end]], axis=1
            )
            spot = lane - (8 * (row ^ place) + 4 * side)
            tail = jnp.where(spot == 0, high[start:middle], tail)
            tail = jnp.where(spot == 1, low[start:middle], tail)
            tail = jnp.where(spot == 2, high[middle:end], tail)
            tail = jnp.where(spot == 3, low[middle:end], tail)
    for flip in range(seq_count):
        target = row ^ flip
        for step in range(3):
            source = target + step - 1
            valid = (source >= 0) & (source < seq_count)
            place = jnp.where(valid, source ^ row, 0)
            for side in range(2):
                piece = jnp.where(valid, total[place, side], 0.0)
                sent[flip][2 * step + side] = piece.astype(jnp.bfloat16)
                if flip == 0:
                    kept[2 * step + side] = jnp.where(first, piece, 0.0)
        sent[flip][6] = tail.astype(jnp.bfloat16)
    kept[6] = jnp.where(first, tail, 0.0)


def total_kernel(kept, *rest):
    arrived, out = rest[:-1], rest[-1]
    total = kept[...]
    for ref in arrived:
        total = total + ref[...].astype(jnp.float32)
    out[...] = total


def beside(cells, cols):
    count = cells.shape[0]
    col = lax.broadcasted_iota(jnp.int32, cells.shape, 0) % cols
    before = jnp.where(col == 0, 0.0, pltpu.roll(cells, 1, 0))
    after = jnp.where(col == cols - 1, 0.0, pltpu.roll(cells, count - 1, 0))
    return [part.astype(jnp.bfloat16) for part in (before, cells, after)]


def decode_kernel(
    lat, feat, cols_dev, seq_count, mine, mate, head_bias, in_weight, in_bias, weight, bias, out
):
    row = lax.axis_index("seq")
    cols = 2 * cols_dev
    sums = mine[6] + mate[6]
    sums = sums + pltpu.roll(sums, 127, 1)
    sums = pltpu.roll(sums, (8 * (17 - row)) % 128, 1)
    lane = lax.broadcasted_iota(jnp.int32, sums.shape, 1)
    biases = jnp.concatenate([head_bias[...], head_bias[...]], axis=1)
    rows = []
    for step in range(3):
        sides = []
        for side in range(2):
            index = 2 * step + side
            upper, lower = (sums[:, 4 * index + at : 4 * index + at + 1] for at in (0, 2))
            rms = jnp.sqrt(jnp.where(lane < lat, upper, lower) / feat + epsilon)
            place = row + step - 1
            valid = (place >= 0) & (place < seq_count)
            latent = jnp.where(valid, (mine[index] + mate[index]) / rms + biases, 0.0)
            sides.append(latent.astype(jnp.bfloat16).astype(jnp.float32))
        rows += [side[:, :lat] for side in sides] + [side[:, lat:] for side in sides]
    wide = jnp.concatenate(beside(jnp.concatenate(rows, axis=0), cols), axis=1)
    deep = 3 * lat
    inner = 4 * cols
    pre = None
    for tap in range(3):
        term = jnp.dot(
            wide[tap * cols : tap * cols + inner],
            in_weight[tap * deep : (tap + 1) * deep, :],
            preferred_element_type=jnp.float32,
        )
        pre = term if pre is None else pre + term
    pre = pre + in_bias[...]
    active = pre / (1.0 + jnp.exp(-pre))
    place = 2 * row - 1 + lax.broadcasted_iota(jnp.int32, active.shape, 0) // cols
    active = jnp.where((place >= 0) & (place < 2 * seq_count), active, 0.0)
    active = active.astype(jnp.bfloat16).astype(jnp.float32)
    shifted = beside(active, cols)
    deep = active.shape[1]
    result = None
    for tap in range(3):
        for col_tap in range(3):
            start = (tap * 3 + col_tap) * deep
            term = jnp.dot(
                shifted[col_tap][tap * cols : (tap + 2) * cols],
                weight[start : start + deep, :],
                preferred_element_type=jnp.float32,
            )
            result = term if result is None else result + term
    out[...] = (result + bias[...]).astype(jnp.bfloat16)


def held(parts):
    return [pltpu.with_memory_space_constraint(part, pltpu.VMEM) for part in parts]


def parked(parts):
    return [pltpu.with_memory_space_constraint(part, pltpu.HBM) for part in parts]


def exchanged(
    queries,
    keys,
    values,
    norm_gain,
    head_weight,
    head_bias,
    in_weight,
    in_bias,
    conv_weight,
    conv_bias,
):
    frame_dev, rows_dev, cols_dev, feat = queries.shape
    seq_count = lax.axis_size("seq")
    blk_count = lax.axis_size("blk")
    lat = head_weight.shape[1]
    wide = in_weight.shape[3]
    out_dev = conv_weight.shape[3]
    tokens = frame_dev * rows_dev * cols_dev
    chips = seq_count * blk_count
    width = feat // chips
    near = [(s, b) for b in range(blk_count) for s in range(seq_count)]
    flips = sorted(near, key=start_rank(seq_count))
    vmem = pl.BlockSpec(memory_space=pltpu.VMEM)
    hbm = pl.BlockSpec(memory_space=pl.ANY)
    flat = [part.reshape(tokens, feat) for part in (queries, keys, values)]
    piece = pltpu.VMEM((3 * tokens, width), jnp.bfloat16)
    *packed, weight, gains = pl.pallas_call(
        lambda *refs: pack_kernel(tokens, width, flips, blk_count, *refs),
        out_shape=[piece] * chips
        + [pltpu.VMEM((lat, width), jnp.bfloat16), pltpu.VMEM((1, width), jnp.float32)],
        in_specs=[hbm] * 5,
        out_specs=[vmem] * (chips + 2),
        scratch_shapes=[
            pltpu.VMEM((3, tokens, feat), jnp.bfloat16),
            pltpu.SemaphoreType.DMA((5,)),
        ],
        compiler_params=pltpu.CompilerParams(vmem_limit_bytes=4 << 20),
        name="pack",
    )(*parked([*flat, head_weight.T, norm_gain.reshape(1, feat)]))
    own = [packed[0]] + [None] * (chips - 1)
    for i in range(1, chips):
        own[i] = lax.ppermute(
            packed[i], ("seq", "blk"), xor_pairs(seq_count, blk_count, *flips[i])
        )
    own[0], in_held, conv_held = pl.pallas_call(
        stage_kernel,
        out_shape=[
            piece,
            pltpu.VMEM((9 * lat, wide), jnp.bfloat16),
            pltpu.VMEM((9 * wide, out_dev), jnp.bfloat16),
        ],
        in_specs=[hbm] * 3,
        out_specs=[hbm] * 3,
        input_output_aliases={0: 0},
        scratch_shapes=[pltpu.SemaphoreType.DMA((2,))],
        compiler_params=pltpu.CompilerParams(vmem_limit_bytes=4 << 20),
        name="stage",
    )(
        *held([own[0]]),
        *parked([in_weight.reshape(9 * lat, wide), conv_weight.reshape(9 * wide, out_dev)]),
    )
    swap = [(0, 1), (1, 0)]
    other = [lax.ppermute(part, "chan", swap) for part in own]
    seat = [flips.index(flip) for flip in near]
    shape = (7, tokens // 2, 128)
    block = pltpu.VMEM((seq_count, 2, tokens // 2, 128), jnp.float32)
    kept, *sent = pl.pallas_call(
        lambda *refs: attend_kernel(tokens, width, seq_count, lat, seat, *refs),
        out_shape=[pltpu.VMEM(shape, jnp.float32)]
        + [pltpu.VMEM(shape, jnp.bfloat16)] * seq_count,
        in_specs=[vmem] * (2 * chips + 2),
        out_specs=[vmem] * (seq_count + 1),
        scratch_shapes=[block],
        compiler_params=pltpu.CompilerParams(vmem_limit_bytes=16 << 20),
        name="attend",
    )(*held(own + other + [weight, gains]))
    arrived = [
        lax.ppermute(sent[flip], ("seq", "blk", "chan"), return_pairs(seq_count, flip))
        for flip in reversed(range(seq_count))
    ]
    mine = pl.pallas_call(
        total_kernel,
        out_shape=pltpu.VMEM(shape, jnp.float32),
        in_specs=[vmem] * (seq_count + 1),
        out_specs=vmem,
        compiler_params=pltpu.CompilerParams(vmem_limit_bytes=4 << 20),
        name="total",
    )(*held([kept, *arrived]))
    mate = lax.ppermute(mine, "chan", swap)
    decoded = pl.pallas_call(
        lambda *refs: decode_kernel(lat, feat, cols_dev, seq_count, *refs),
        out_shape=jax.ShapeDtypeStruct((2 * tokens, out_dev), jnp.bfloat16),
        in_specs=[vmem] * 7,
        out_specs=vmem,
        compiler_params=pltpu.CompilerParams(vmem_limit_bytes=16 << 20),
        name="decode",
    )(
        *held(
            [
                mine,
                mate,
                head_bias.reshape(1, lat),
                in_held,
                in_bias.reshape(1, wide),
                conv_held,
                conv_bias.reshape(1, out_dev),
            ]
        )
    )
    return decoded.reshape(frame_dev, rows_dev, 2 * cols_dev, out_dev)


def per_device(queries, *rest):
    frame_dev, rows_dev, cols_dev, feat = queries.shape
    seq_count = lax.axis_size("seq")
    blk_count = lax.axis_size("blk")
    lat = rest[3].shape[1]
    fits = (
        frame_dev == 1
        and rows_dev == 2
        and cols_dev % 16 == 0
        and lat == 64
        and blk_count == 2
        and seq_count & (seq_count - 1) == 0
        and lax.axis_size("chan") == 2
        and feat // HD % (seq_count * blk_count) == 0
        and 8 * seq_count <= 128
    )
    return (exchanged if fits else gathered)(queries, *rest)


def solution(mesh):
    return jax.shard_map(
        per_device,
        mesh=mesh,
        in_specs=(
            P(("groups", "blk"), "seq", "chan", None),
            P(("groups", "blk"), "seq", "chan", None),
            P(("groups", "blk"), "seq", "chan", None),
            P(),
            P(),
            P(),
            P(),
            P(),
            P(None, None, None, "chan"),
            P("chan"),
        ),
        out_specs=P(("groups", "blk"), "seq", None, "chan"),
        check_vma=False,
    )
```

```python
import jax
import jax.numpy as jnp
from jax import lax
from jax.experimental import pallas as pl
from jax.experimental.pallas import tpu as pltpu
from jax.sharding import PartitionSpec as P

HD = 128


epsilon = 1e-06


def with_halo(cells, sides, width):
    for axis, dim in sides:
        count = lax.axis_size(axis)
        ends = count - 1
        head = lax.slice_in_dim(cells, 0, width, axis=dim)
        tail = lax.slice_in_dim(cells, cells.shape[dim] - width, cells.shape[dim], axis=dim)
        cells = jnp.concatenate(
            [
                lax.ppermute(tail, axis, [(i, (i + 1) % count) for i in range(ends)]),
                cells,
                lax.ppermute(head, axis, [((i + 1) % count, i) for i in range(ends)]),
            ],
            axis=dim,
        )
    return cells


def conv_valid(inputs, kernel):
    col_count = inputs.shape[2]
    padded = jnp.pad(inputs, ((0, 0), (0, 0), (1, 1), (0, 0)))
    stacked = jnp.concatenate(
        [padded[:, :, col_tap : col_tap + col_count, :] for col_tap in range(3)], axis=-1
    )
    rows_out = inputs.shape[1] - 2
    result = None
    for row_tap in range(3):
        flat_kernel = kernel[row_tap].reshape(3 * kernel.shape[2], kernel.shape[3])
        term = jnp.einsum(
            "frci,io->frco",
            stacked[:, row_tap : row_tap + rows_out],
            flat_kernel,
            preferred_element_type=jnp.float32,
        )
        result = term if result is None else result + term
    return result


def absorb(running, key_block, value_block, query_heads, score_scale):
    run_max, denoms, numers = running
    scores = (
        jnp.einsum("hqd,hkd->hqk", query_heads, key_block, preferred_element_type=jnp.float32)
        * score_scale
    )
    fresh_max = jnp.maximum(run_max, jnp.max(scores, axis=-1))
    rescale = jnp.exp(run_max - fresh_max)
    expo = jnp.exp(scores - fresh_max[..., None])
    denoms = denoms * rescale + jnp.sum(expo, axis=-1)
    numers = numers * rescale[..., None] + jnp.einsum(
        "hqk,hkd->hqd", expo.astype(jnp.bfloat16), value_block, preferred_element_type=jnp.float32
    )
    return (fresh_max, denoms, numers)


def decode(wide_rows, rows_dev, in_weight, in_bias, conv_weight, conv_bias):
    pre_act = conv_valid(wide_rows, in_weight) + in_bias
    row_ids = lax.axis_index("seq") * rows_dev - 1 + jnp.arange(rows_dev + 2, dtype=jnp.int32)
    inside = (row_ids >= 0) & (row_ids < rows_dev * lax.axis_size("seq"))
    activation = jnp.where(inside[None, :, None, None], jax.nn.silu(pre_act), 0.0).astype(
        jnp.bfloat16
    )
    return (conv_valid(activation, conv_weight) + conv_bias).astype(jnp.bfloat16)


def gathered(
    queries,
    keys,
    values,
    norm_gain,
    head_weight,
    head_bias,
    in_weight,
    in_bias,
    conv_weight,
    conv_bias,
):
    frame_dev, rows_dev, cols_dev, feat = queries.shape
    seq_count = lax.axis_size("seq")
    feat_dev = feat // seq_count
    heads_dev = feat_dev // HD
    score_scale = HD ** (-0.5)
    query_all, key_all, value_all = (
        lax.all_to_all(queries, "seq", split_axis=3, concat_axis=1, tiled=True),
        lax.all_to_all(keys, "seq", split_axis=3, concat_axis=1, tiled=True),
        lax.all_to_all(values, "seq", split_axis=3, concat_axis=1, tiled=True),
    )
    all_rows = query_all.shape[1]

    def to_heads(block):
        return block.reshape(-1, heads_dev, HD).transpose(1, 0, 2)

    query_heads = to_heads(query_all)
    key_heads = to_heads(key_all)
    value_heads = to_heads(value_all)
    token_local = query_heads.shape[1]

    def attend_piece(running, block_pair):
        key_piece, value_piece = block_pair
        key_rows = key_piece.shape[1]
        if key_rows > 1024 and key_rows % 1024 == 0:
            count = key_rows // 1024
            key_split = key_piece.reshape(heads_dev, count, 1024, HD).transpose(1, 0, 2, 3)
            value_split = value_piece.reshape(heads_dev, count, 1024, HD).transpose(1, 0, 2, 3)

            def step_block(state, pair_block):
                return (absorb(state, pair_block[0], pair_block[1], query_heads, score_scale), None)

            running, _ = lax.scan(step_block, running, (key_split, value_split))
            return running
        return absorb(running, key_piece, value_piece, query_heads, score_scale)

    start_state = (
        jnp.full((heads_dev, token_local), -1e30, jnp.float32),
        jnp.zeros((heads_dev, token_local), jnp.float32),
        jnp.zeros((heads_dev, token_local, HD), jnp.float32),
    )
    run_max, denoms, numers = attend_piece(
        start_state,
        (
            lax.all_gather(key_heads, ("blk", "chan"), axis=1, tiled=True),
            lax.all_gather(value_heads, ("blk", "chan"), axis=1, tiled=True),
        ),
    )
    attended = (numers / denoms[..., None]).astype(jnp.bfloat16)
    attended = attended.transpose(1, 0, 2).reshape(frame_dev, all_rows, cols_dev, feat_dev)
    back = lax.all_to_all(attended, "seq", split_axis=1, concat_axis=3, tiled=True)
    wide_att = back.astype(jnp.float32)
    squares = jnp.sum(wide_att * wide_att, axis=-1)
    normed = (wide_att * norm_gain).astype(jnp.bfloat16)
    projected = jnp.einsum("frcd,dl->frcl", normed, head_weight, preferred_element_type=jnp.float32)
    rms = jnp.sqrt(squares / feat + epsilon)
    latent_cols = (projected / rms[..., None] + head_bias).astype(jnp.bfloat16)
    latent = lax.all_gather(latent_cols, "chan", axis=2, tiled=True)
    wide_rows = with_halo(latent, (("seq", 1),), 2)
    return decode(wide_rows, rows_dev, in_weight, in_bias, conv_weight, conv_bias)


def xor_pairs(seq_count, blk_count, row_flip, blk_flip):
    return [
        (s * blk_count + b, (s ^ row_flip) * blk_count + (b ^ blk_flip))
        for s in range(seq_count)
        for b in range(blk_count)
    ]


def start_rank(seq_count):
    def rank(flip):
        row_flip, blk_flip = flip
        far = row_flip > seq_count // 2
        late = 2 if far else (0 if row_flip == seq_count // 2 else 1)
        return (flip != (0, 0), late, -blk_flip if far else row_flip + blk_flip, -row_flip)

    return rank


def return_pairs(seq_count, flip):
    pairs = []
    for s in range(seq_count):
        for b in range(2):
            for core in range(2):
                if flip or core:
                    target = ((s ^ flip) * 2 + (b ^ core)) * 2 + core
                    pairs.append(((s * 2 + b) * 2 + core, target))
    return pairs


def pack_kernel(tokens, width, flips, blk_count, *refs):
    sources, head_t, gain = refs[:3], refs[3], refs[4]
    outs, weight, gains, whole, sems = refs[5:-4], refs[-4], refs[-3], refs[-2], refs[-1]
    row = lax.axis_index("seq")
    blk = lax.axis_index("blk")
    start = pl.multiple_of((row * blk_count + blk) * width, 128)
    copies = [(source, whole.at[part]) for part, source in enumerate(sources)]
    copies.append((head_t.at[:, pl.ds(start, width)], weight))
    copies.append((gain.at[:, pl.ds(start, width)], gains))
    copies = [
        pltpu.make_async_copy(source, out, sems.at[i]) for i, (source, out) in enumerate(copies)
    ]
    for copy in copies:
        copy.start()
    for part, copy in enumerate(copies):
        copy.wait()
        if part < 3:
            for place, (row_flip, blk_flip) in enumerate(flips):
                target = (row ^ row_flip) * blk_count + (blk ^ blk_flip)
                begin = pl.multiple_of(target * width, 128)
                outs[place][part * tokens : (part + 1) * tokens, :] = whole[
                    part, :, pl.ds(begin, width)
                ]


def stage_kernel(first, in_weight, weight, same, in_copy, copy, sems):
    del first, same
    moves = [
        pltpu.make_async_copy(source, out, sems.at[i])
        for i, (source, out) in enumerate(((in_weight, in_copy), (weight, copy)))
    ]
    for move in moves:
        move.start()
    for move in moves:
        move.wait()


def attend_kernel(tokens, width, seq_count, lat, seat, *refs):
    count = 2 * seq_count
    own = [refs[i] for i in seat]
    other = [refs[count + i] for i in seat]
    weight, gains, kept = refs[2 * count : 2 * count + 3]
    sent, total = refs[2 * count + 3 : -1], refs[-1]
    row = lax.axis_index("seq")
    first = lax.axis_index("chan") == 0
    factor = HD ** (-0.5) * 1.4426950408889634
    spans = [slice(head * HD, (head + 1) * HD) for head in range(width // HD)]
    scores = []
    for span in spans:
        queries = []
        for near, far in zip(range(seq_count), range(seq_count, count)):
            queries.append(jnp.where(first, own[near][:tokens, span], other[far][:tokens, span]))
            queries.append(jnp.where(first, other[near][:tokens, span], own[far][:tokens, span]))
        query = jnp.concatenate(queries, axis=0)
        key = jnp.concatenate([ref[tokens : 2 * tokens, span] for ref in own + other], axis=0)
        scores.append(
            lax.dot_general(
                query, key, (((1,), (1,)), ((), ())), preferred_element_type=jnp.float32
            )
        )
    tops = [jnp.max(score, axis=-1, keepdims=True) for score in scores]
    expos = [jnp.exp2((score - top) * factor) for score, top in zip(scores, tops)]
    denoms = [jnp.sum(expo, axis=-1, keepdims=True) for expo in expos]
    numers = [
        jnp.dot(
            expo.astype(jnp.bfloat16),
            jnp.concatenate([ref[2 * tokens :, span] for ref in own + other], axis=0),
            preferred_element_type=jnp.float32,
        )
        for expo, span in zip(expos, spans)
    ]
    attended = [
        (numer / denom).astype(jnp.bfloat16).astype(jnp.float32)
        for numer, denom in zip(numers, denoms)
    ]
    squares = sum(part * part for part in attended)
    normed = jnp.concatenate(
        [(part * gains[:, span]).astype(jnp.bfloat16) for part, span in zip(attended, spans)],
        axis=1,
    )
    projected = lax.dot_general(
        normed, weight[...], (((1,), (1,)), ((), ())), preferred_element_type=jnp.float32
    )
    half = tokens // 2
    lane = lax.broadcasted_iota(jnp.int32, (half, 128), 1)
    squares = jnp.broadcast_to(jnp.sum(squares, axis=-1, keepdims=True), squares.shape)
    high = squares.astype(jnp.bfloat16).astype(jnp.float32)
    low = squares - high
    tail = jnp.zeros((half, 128), jnp.float32)
    for place in range(seq_count):
        for side in range(2):
            start = (2 * place + side) * tokens
            middle, end = start + half, start + tokens
            total[place, side] = jnp.concatenate(
                [projected[start:middle], projected[middle:end]], axis=1
            )
            spot = lane - (8 * (row ^ place) + 4 * side)
            tail = jnp.where(spot == 0, high[start:middle], tail)
            tail = jnp.where(spot == 1, low[start:middle], tail)
            tail = jnp.where(spot == 2, high[middle:end], tail)
            tail = jnp.where(spot == 3, low[middle:end], tail)
    for flip in range(seq_count):
        target = row ^ flip
        for step in range(3):
            source = target + step - 1
            valid = (source >= 0) & (source < seq_count)
            place = jnp.where(valid, source ^ row, 0)
            for side in range(2):
                piece = jnp.where(valid, total[place, side], 0.0)
                sent[flip][2 * step + side] = piece.astype(jnp.bfloat16)
                if flip == 0:
                    kept[2 * step + side] = jnp.where(first, piece, 0.0)
        sent[flip][6] = tail.astype(jnp.bfloat16)
    kept[6] = jnp.where(first, tail, 0.0)


def total_kernel(kept, *rest):
    arrived, out = rest[:-1], rest[-1]
    total = kept[...]
    for ref in arrived:
        total = total + ref[...].astype(jnp.float32)
    out[...] = total


def beside(cells, cols):
    count = cells.shape[0]
    col = lax.broadcasted_iota(jnp.int32, cells.shape, 0) % cols
    before = jnp.where(col == 0, 0.0, pltpu.roll(cells, 1, 0))
    after = jnp.where(col == cols - 1, 0.0, pltpu.roll(cells, count - 1, 0))
    return [part.astype(jnp.bfloat16) for part in (before, cells, after)]


def decode_kernel(
    lat, feat, cols_dev, seq_count, mine, mate, head_bias, in_weight, in_bias, weight, bias, out
):
    row = lax.axis_index("seq")
    cols = 2 * cols_dev
    sums = mine[6] + mate[6]
    sums = sums + pltpu.roll(sums, 127, 1)
    sums = pltpu.roll(sums, (8 * (17 - row)) % 128, 1)
    lane = lax.broadcasted_iota(jnp.int32, sums.shape, 1)
    biases = jnp.concatenate([head_bias[...], head_bias[...]], axis=1)
    rows = []
    for step in range(3):
        sides = []
        for side in range(2):
            index = 2 * step + side
            upper, lower = (sums[:, 4 * index + at : 4 * index + at + 1] for at in (0, 2))
            rms = jnp.sqrt(jnp.where(lane < lat, upper, lower) / feat + epsilon)
            place = row + step - 1
            valid = (place >= 0) & (place < seq_count)
            latent = jnp.where(valid, (mine[index] + mate[index]) / rms + biases, 0.0)
            sides.append(latent.astype(jnp.bfloat16).astype(jnp.float32))
        rows += [side[:, :lat] for side in sides] + [side[:, lat:] for side in sides]
    wide = jnp.concatenate(beside(jnp.concatenate(rows, axis=0), cols), axis=1)
    deep = 3 * lat
    inner = 4 * cols
    pre = None
    for tap in range(3):
        term = jnp.dot(
            wide[tap * cols : tap * cols + inner],
            in_weight[tap * deep : (tap + 1) * deep, :],
            preferred_element_type=jnp.float32,
        )
        pre = term if pre is None else pre + term
    pre = pre + in_bias[...]
    active = pre / (1.0 + jnp.exp(-pre))
    place = 2 * row - 1 + lax.broadcasted_iota(jnp.int32, active.shape, 0) // cols
    active = jnp.where((place >= 0) & (place < 2 * seq_count), active, 0.0)
    active = active.astype(jnp.bfloat16).astype(jnp.float32)
    shifted = beside(active, cols)
    deep = active.shape[1]
    result = None
    for tap in range(3):
        for col_tap in range(3):
            start = (tap * 3 + col_tap) * deep
            term = jnp.dot(
                shifted[col_tap][tap * cols : (tap + 2) * cols],
                weight[start : start + deep, :],
                preferred_element_type=jnp.float32,
            )
            result = term if result is None else result + term
    out[...] = (result + bias[...]).astype(jnp.bfloat16)


def held(parts):
    return [pltpu.with_memory_space_constraint(part, pltpu.VMEM) for part in parts]


def parked(parts):
    return [pltpu.with_memory_space_constraint(part, pltpu.HBM) for part in parts]


def exchanged(
    queries,
    keys,
    values,
    norm_gain,
    head_weight,
    head_bias,
    in_weight,
    in_bias,
    conv_weight,
    conv_bias,
):
    frame_dev, rows_dev, cols_dev, feat = queries.shape
    seq_count = lax.axis_size("seq")
    blk_count = lax.axis_size("blk")
    lat = head_weight.shape[1]
    wide = in_weight.shape[3]
    out_dev = conv_weight.shape[3]
    tokens = frame_dev * rows_dev * cols_dev
    chips = seq_count * blk_count
    width = feat // chips
    near = [(s, b) for b in range(blk_count) for s in range(seq_count)]
    flips = sorted(near, key=start_rank(seq_count))
    vmem = pl.BlockSpec(memory_space=pltpu.VMEM)
    hbm = pl.BlockSpec(memory_space=pl.ANY)
    flat = [part.reshape(tokens, feat) for part in (queries, keys, values)]
    piece = pltpu.VMEM((3 * tokens, width), jnp.bfloat16)
    *packed, weight, gains = pl.pallas_call(
        lambda *refs: pack_kernel(tokens, width, flips, blk_count, *refs),
        out_shape=[piece] * chips
        + [pltpu.VMEM((lat, width), jnp.bfloat16), pltpu.VMEM((1, width), jnp.float32)],
        in_specs=[hbm] * 5,
        out_specs=[vmem] * (chips + 2),
        scratch_shapes=[
            pltpu.VMEM((3, tokens, feat), jnp.bfloat16),
            pltpu.SemaphoreType.DMA((5,)),
        ],
        compiler_params=pltpu.CompilerParams(vmem_limit_bytes=4 << 20),
        name="pack",
    )(*parked([*flat, head_weight.T, norm_gain.reshape(1, feat)]))
    own = [packed[0]] + [None] * (chips - 1)
    for i in range(1, chips):
        own[i] = lax.ppermute(
            packed[i], ("seq", "blk"), xor_pairs(seq_count, blk_count, *flips[i])
        )
    own[0], in_held, conv_held = pl.pallas_call(
        stage_kernel,
        out_shape=[
            piece,
            pltpu.VMEM((9 * lat, wide), jnp.bfloat16),
            pltpu.VMEM((9 * wide, out_dev), jnp.bfloat16),
        ],
        in_specs=[hbm] * 3,
        out_specs=[hbm] * 3,
        input_output_aliases={0: 0},
        scratch_shapes=[pltpu.SemaphoreType.DMA((2,))],
        compiler_params=pltpu.CompilerParams(vmem_limit_bytes=4 << 20),
        name="stage",
    )(
        *held([own[0]]),
        *parked([in_weight.reshape(9 * lat, wide), conv_weight.reshape(9 * wide, out_dev)]),
    )
    swap = [(0, 1), (1, 0)]
    other = [lax.ppermute(part, "chan", swap) for part in own]
    seat = [flips.index(flip) for flip in near]
    shape = (7, tokens // 2, 128)
    block = pltpu.VMEM((seq_count, 2, tokens // 2, 128), jnp.float32)
    kept, *sent = pl.pallas_call(
        lambda *refs: attend_kernel(tokens, width, seq_count, lat, seat, *refs),
        out_shape=[pltpu.VMEM(shape, jnp.float32)]
        + [pltpu.VMEM(shape, jnp.bfloat16)] * seq_count,
        in_specs=[vmem] * (2 * chips + 2),
        out_specs=[vmem] * (seq_count + 1),
        scratch_shapes=[block],
        compiler_params=pltpu.CompilerParams(vmem_limit_bytes=16 << 20),
        name="attend",
    )(*held(own + other + [weight, gains]))
    arrived = [
        lax.ppermute(sent[flip], ("seq", "blk", "chan"), return_pairs(seq_count, flip))
        for flip in reversed(range(seq_count))
    ]
    mine = pl.pallas_call(
        total_kernel,
        out_shape=pltpu.VMEM(shape, jnp.float32),
        in_specs=[vmem] * (seq_count + 1),
        out_specs=vmem,
        compiler_params=pltpu.CompilerParams(vmem_limit_bytes=4 << 20),
        name="total",
    )(*held([kept, *arrived]))
    mate = lax.ppermute(mine, "chan", swap)
    decoded = pl.pallas_call(
        lambda *refs: decode_kernel(lat, feat, cols_dev, seq_count, *refs),
        out_shape=jax.ShapeDtypeStruct((2 * tokens, out_dev), jnp.bfloat16),
        in_specs=[vmem] * 7,
        out_specs=vmem,
        compiler_params=pltpu.CompilerParams(vmem_limit_bytes=16 << 20),
        name="decode",
    )(
        *held(
            [
                mine,
                mate,
                head_bias.reshape(1, lat),
                in_held,
                in_bias.reshape(1, wide),
                conv_held,
                conv_bias.reshape(1, out_dev),
            ]
        )
    )
    return decoded.reshape(frame_dev, rows_dev, 2 * cols_dev, out_dev)


def per_device(queries, *rest):
    frame_dev, rows_dev, cols_dev, feat = queries.shape
    seq_count = lax.axis_size("seq")
    blk_count = lax.axis_size("blk")
    lat = rest[3].shape[1]
    fits = (
        frame_dev == 1
        and rows_dev == 2
        and cols_dev % 16 == 0
        and lat == 64
        and blk_count == 2
        and seq_count & (seq_count - 1) == 0
        and lax.axis_size("chan") == 2
        and feat // HD % (seq_count * blk_count) == 0
        and 8 * seq_count <= 128
    )
    return (exchanged if fits else gathered)(queries, *rest)


def solution(mesh):
    return jax.shard_map(
        per_device,
        mesh=mesh,
        in_specs=(
            P(("groups", "blk"), "seq", "chan", None),
            P(("groups", "blk"), "seq", "chan", None),
            P(("groups", "blk"), "seq", "chan", None),
            P(),
            P(),
            P(),
            P(),
            P(),
            P(None, None, None, "chan"),
            P("chan"),
        ),
        out_specs=P(("groups", "blk"), "seq", None, "chan"),
        check_vma=False,
    )
```
